32 devices in a mesh: basin: 4 (over y, x), tile: 8 (over z, core).
Axes of the slice: x: 2, y: 2, z: 4, core: 2. Of those that a mesh axis runs over, the one named last changes fastest.
Arguments:
- depth_start: float32 [4, 512, 512], P('basin', 'tile'), may hold values from -6 to 6
- roughness: float32 [4, 512, 512], P('basin', 'tile'), may hold values from 0.025 to 0.25
- depth_seed: float32 [4, 512, 512], P('basin', 'tile'), may hold values from -6 to 6
- zone_label: int32 [4, 512, 512], P('basin', 'tile'), may hold values from 0 to 32511, as said below
- owner_slot: int32 [32512], replicated, may hold values from 0 to 32511, each once
- retention: float32 [128, 1024], P('basin', 'tile'), may hold values from 0 to 1
- forcing: float32 [128, 1024], P('basin', 'tile'), may hold values from -0.6 to 0.6
- levee_cell: int32 [128, 1024], P('basin', 'tile'), may hold values from 0 to 32767
Outputs:
- zone_gradient: float32 [32512], P(('basin', 'tile'))
- zone_curvature: float32 [32512], P(('basin', 'tile'))
- reach_adjoint: float32 [128, 1024], P('basin', 'tile')
The draws below stay inside these ranges and needn't reach their ends.
Inputs may be any that keep to these rules, and one draw needn't show every extreme that they name: `zone_label`: seven cells in eight of the rows b, (t * 64) to (t * 64 + 63) take zones of the band (b * 8 + t) * 1016 onward, 1016 wide, lower ones more often; the others any zone. `owner_slot`: each zone once. `levee_cell`: Row-major index of a cell within rows (j // 128) * 64 to (j // 128) * 64 + 63 of basin i // 32.
All inputs are finite; a program needn't handle non-finite values.
Results may differ from the reference program's by a relative error of at most 0.0003.
Values sent between devices are 32-bit elements; how exact they have to be, the bound alone decides.
A program may use at most 64 MiB of HBM per device.

```python
import math
import jax
import jax.numpy as jnp
from jax import lax

R = 64
C = 512
L_DEV = 32
CH_DEV = 128
ZONES = 32512
STEPS = 4
BASINS = 4
TILES = 8
ROWS = 512
CHANNEL_SEGMENTS = 128
CHAINS = 1024
ZONE_SPAN = 1016


def draw_zone_label(key, part):
    key_first, key_second, key_stray, key_pick = jax.random.split(jax.random.fold_in(key, 17), 4)
    shape = (BASINS, ROWS, C)
    basin_index = lax_free_iota(shape, 0)
    row_index = lax_free_iota(shape, 1)
    block_index = basin_index * TILES + row_index // R
    offset = jnp.minimum(jax.random.randint(key_first, shape, 0, ZONE_SPAN), jax.random.randint(key_second, shape, 0, ZONE_SPAN))
    home_zone = block_index * ZONE_SPAN + offset
    stray_zone = jax.random.randint(key_stray, shape, 0, ZONES)
    picked = jax.random.randint(key_pick, shape, 0, 8) == 0
    return jnp.where(picked, stray_zone, home_zone).astype(jnp.int32)


def lax_free_iota(shape, axis_number):
    sizes = [1] * len(shape)
    sizes[axis_number] = shape[axis_number]
    return jnp.broadcast_to(jnp.arange(shape[axis_number], dtype=jnp.int32).reshape(sizes), shape)


def draw_retention(key, part):
    key_chain_rates, key_perturbation, key_surge, key_multiplier = jax.random.split(jax.random.fold_in(key, 29), 4)
    lowest = 0.3 / CHANNEL_SEGMENTS
    highest = 1.0 / 30.0
    reach_chain_rates = jnp.exp(jax.random.uniform(key_chain_rates, (1, CHAINS), jnp.float32, math.log(lowest), math.log(highest)))
    perturbation = jax.random.uniform(key_perturbation, (CHANNEL_SEGMENTS, CHAINS), jnp.float32, 0.5, 2.0)
    surge_rows = jax.random.uniform(key_surge, (CHANNEL_SEGMENTS, 1), jnp.float32) < 3.0 / CHANNEL_SEGMENTS
    multiplier = jax.random.uniform(key_multiplier, (CHANNEL_SEGMENTS, 1), jnp.float32, 0.5, 0.8)
    kept_fraction = jnp.exp(-reach_chain_rates * perturbation) * jnp.where(surge_rows, multiplier, 1.0)
    return kept_fraction.astype(jnp.float32)


def place_ends(array, rng, smallest, largest):
    longest = array.shape.index(max(array.shape))
    spots = []
    for shift in (0, 1):
        where = [jax.random.randint(jax.random.fold_in(rng, axis), (), 0, length) for axis, length in enumerate(array.shape)]
        where[longest] = (where[longest] + shift) % array.shape[longest]
        spots.append(tuple(where))
    return array.at[spots[0]].set(smallest).at[spots[1]].set(largest)


def block_scale(rng, extent, pieces, least, largest):
    level = 1.0
    for dim, blocks in pieces:
        steps = jax.random.uniform(jax.random.fold_in(jax.random.fold_in(rng, 6), dim), (blocks,), jnp.float32, least / len(pieces), largest / len(pieces))
        level = level * jnp.repeat(jnp.exp(steps), extent[dim] // blocks).reshape((-1,) + (1,) * (len(extent) - 1 - dim))
    return level


def bell_draw(rng, shape, width, most, pieces=(), held_as=jnp.bfloat16):
    entries = width * jax.random.normal(rng, shape, jnp.float32)
    if pieces:
        entries = entries * block_scale(rng, shape, pieces, -0.22, 0.18)
    return jnp.clip(entries, -most, most).astype(held_as)


def setup_inputs(seed: int = 0) -> dict:
    arg_keys = jax.random.split(jax.random.key(seed), 9)
    return {
        "depth_start": bell_draw(arg_keys[0], (BASINS, ROWS, C), 1.0, 6.0, ((0, 4), (1, 8)), jnp.float32),
        "roughness": jnp.clip(jnp.exp(math.log(0.25) - 2.3025851 * jax.random.uniform(arg_keys[1], (BASINS, ROWS, C), jnp.float32) ** block_scale(arg_keys[1], (BASINS, ROWS, C), ((0, 4), (1, 8)), -0.2, 0.2)), 0.025, 0.25),
        "depth_seed": bell_draw(arg_keys[2], (BASINS, ROWS, C), 1.0, 6.0, ((0, 4), (1, 8)), jnp.float32),
        "zone_label": draw_zone_label(jax.random.fold_in(arg_keys[8], 71), 0),
        "owner_slot": jax.random.permutation(arg_keys[4], ZONES).astype(jnp.int32),
        "retention": draw_retention(jax.random.fold_in(arg_keys[8], 71), 0),
        "forcing": bell_draw(arg_keys[6], (CHANNEL_SEGMENTS, CHAINS), 0.1, 0.6, ((0, 4), (1, 8)), jnp.float32),
        "levee_cell": place_ends(jax.random.randint(arg_keys[7], (CHANNEL_SEGMENTS, CHAINS), 0, R * C), jax.random.fold_in(arg_keys[7], 1), 0, (R * C) - 1).astype(jnp.int32),
    }


courant = 0.24
rough_ref = 0.025
levee_gain = 0.1


def neighbours(padded):
    return [padded[2:, 1:-1], padded[:-2, 1:-1], padded[1:-1, 2:], padded[1:-1, :-2]]


def face_weights(conduct_pad):
    centre = conduct_pad[1:-1, 1:-1]
    return [jnp.where((centre > 0) & (opposite > 0), 0.5 * (centre + opposite), 0.0) for opposite in neighbours(conduct_pad)]


def spread(field_pad, face_list):
    centre = field_pad[1:-1, 1:-1]
    accumulated = jnp.zeros(centre.shape, jnp.float32)
    for weight, opposite in zip(face_list, neighbours(field_pad)):
        accumulated = accumulated + weight * (opposite - centre)
    return accumulated


def product_terms(depth_pad, adjoint_pad, face_list):
    depth_centre = depth_pad[1:-1, 1:-1]
    adjoint_centre = adjoint_pad[1:-1, 1:-1]
    accumulated = jnp.zeros(depth_centre.shape, jnp.float32)
    for weight, depth_near, adjoint_near in zip(face_list, neighbours(depth_pad), neighbours(adjoint_pad)):
        accumulated = accumulated + jnp.where(weight > 0, (depth_near - depth_centre) * (adjoint_near - adjoint_centre), 0.0)
    return accumulated


def basin_pass(depth_zero, rough_cells, seed_cells):
    conductance = rough_ref / rough_cells
    face_list = face_weights(jnp.pad(conductance, 1))
    states = [depth_zero]
    for section_index in range(STEPS - 1):
        states.append(states[-1] + courant * spread(jnp.pad(states[-1], 1), face_list))
    adjoint = seed_cells
    accumulated = jnp.zeros(depth_zero.shape, jnp.float32)
    for section_index in reversed(range(STEPS)):
        adjoint_pad = jnp.pad(adjoint, 1)
        accumulated = accumulated + product_terms(jnp.pad(states[section_index], 1), adjoint_pad, face_list)
        adjoint = adjoint + courant * spread(adjoint_pad, face_list)
    return adjoint, 0.5 * courant * conductance * accumulated


def reference(depth_start, roughness, depth_seed, zone_label, owner_slot, retention, forcing, levee_cell):
    def per_basin(sums, inputs):
        depth_zero, rough_cells, seed_cells, label_cells = inputs
        adjoint, cell_gradient = basin_pass(depth_zero, rough_cells, seed_cells)
        slot_ids = owner_slot[label_cells].reshape(-1)
        flat_grad = cell_gradient.reshape(-1)
        grad_sum = sums[0] + jax.ops.segment_sum(flat_grad, slot_ids, num_segments=ZONES)
        curv_sum = sums[1] + jax.ops.segment_sum(flat_grad * flat_grad, slot_ids, num_segments=ZONES)
        return (grad_sum, curv_sum), adjoint

    start_sums = (jnp.zeros((ZONES,), jnp.float32), jnp.zeros((ZONES,), jnp.float32))
    (zone_gradient, zone_curvature), adjoints = lax.scan(per_basin, start_sums, (depth_start, roughness, depth_seed, zone_label))
    blocks = adjoints.reshape(BASINS, TILES, R * C)
    basin_index = (jnp.arange(CHANNEL_SEGMENTS, dtype=jnp.int32) // L_DEV)[:, None]
    tile_index = (jnp.arange(CHAINS, dtype=jnp.int32) // CH_DEV)[None, :]
    levee_value = blocks[basin_index, tile_index, levee_cell]
    drive_term = forcing + levee_gain * levee_value

    def upstream(downstream, reach_row):
        keep_rate, inflow = reach_row
        updated = keep_rate * downstream + inflow
        return updated, updated

    last_value, reach_adjoint = lax.scan(upstream, jnp.zeros((CHAINS,), jnp.float32), (retention, drive_term), reverse=True)
    return zone_gradient, zone_curvature, reach_adjoint
```

```python
import functools

import jax
import jax.numpy as jnp
from jax import lax
from jax.experimental import pallas as pl
from jax.experimental.pallas import tpu as pltpu
from jax.sharding import PartitionSpec as P

STEPS = 4
HALO = 8
LANES = 128
ROWS_AT_ONCE = 8

courant = 0.24
rough_ref = 0.025
levee_gain = 0.1

F32 = jnp.float32
BF16 = jnp.bfloat16
I32 = jnp.int32
MESH = pl.DeviceIdType.MESH


def round_up(value, unit):
    return -(-value // unit) * unit


def iota(shape, dim):
    return lax.broadcasted_iota(I32, shape, dim)


def nt_dot(left, right):
    return lax.dot_general(
        left, right, (((1,), (1,)), ((), ())), preferred_element_type=F32
    )


def kernel(
    nb, nt, span, gp, digits,
    depth_in, rough_in, seed_in, label_hbm, owner_hbm, keep_hbm, force_hbm, cell_hbm,
    packed_out,
    label_in, owner_in, keep_in, force_in, cell_in, ext, table, owner_f, slot_s, pieces, diff_e, diff_s, adj_f, adj0, levee,
    hist, sums, pair, part, recv2, maps,
    halo_send, halo_recv, map_send, map_recv, one_send, one_recv, two_send, two_recv, load_sem,
):
    b = lax.axis_index("basin")
    t = lax.axis_index("tile")
    rows, cols = depth_in.shape
    label_groups = table.shape[1] // (1 + digits)
    groups = nb * nt * gp

    blocks = nb * nt // 2
    side = lax.rem(t, 2)
    mine = b * (nt // 2) + t // 2

    def peer(k):
        other = lax.rem(mine + k, blocks)
        return other, (other // (nt // 2), 2 * lax.rem(other, nt // 2) + side)

    barrier = pltpu.get_barrier_semaphore()
    for k in range(1, blocks):
        pl.semaphore_signal(barrier, inc=1, device_id=peer(k)[1], device_id_type=MESH)
    near = sorted({1, nt - 1})
    for k in near:
        pl.semaphore_signal(
            barrier, inc=1, device_id=(b, lax.rem(t + k, nt)), device_id_type=MESH
        )

    fields = (depth_in, rough_in, seed_in)
    pairs = (
        (depth_in, ext.at[0, pl.ds(HALO, rows)]), (rough_in, ext.at[1, pl.ds(HALO, rows)]),
        (seed_in, ext.at[2, pl.ds(HALO, rows)]),
        (owner_hbm, owner_in), (label_hbm, label_in),
        (cell_hbm, cell_in), (keep_hbm, keep_in), (force_hbm, force_in),
    )
    loads = [
        pltpu.make_async_copy(source, target, load_sem.at[index])
        for index, (source, target) in enumerate(pairs)
    ]
    for load in loads:
        load.start()

    def down_copy(f):
        return pltpu.make_async_remote_copy(
            src_ref=fields[f].at[pl.ds(rows - HALO, HALO)],
            dst_ref=ext.at[f, pl.ds(0, HALO)],
            send_sem=halo_send.at[0, f],
            recv_sem=halo_recv.at[0, f],
            device_id=(b, lax.rem(t + 1, nt)),
            device_id_type=MESH,
        )

    def up_copy(f):
        return pltpu.make_async_remote_copy(
            src_ref=fields[f].at[pl.ds(0, HALO)],
            dst_ref=ext.at[f, pl.ds(HALO + rows, HALO)],
            send_sem=halo_send.at[1, f],
            recv_sem=halo_recv.at[1, f],
            device_id=(b, lax.rem(t + nt - 1, nt)),
            device_id_type=MESH,
        )

    def start_halos():
        @pl.when(t < nt - 1)
        def _():
            for f in range(3):
                down_copy(f).start()

        @pl.when(t > 0)
        def _():
            for f in range(3):
                up_copy(f).start()

    def right(v):
        return pltpu.roll(v, cols - 1, 1)

    def from_left(v):
        return pltpu.roll(v, 1, 1)

    def sweep(depth, rough, adjoint, mask_rows):
        deep = depth.shape[0]
        face_e = iota((deep, cols), 1) < cols - 1

        def below(v):
            return pltpu.roll(v, deep - 1, 0)

        def from_above(v):
            return pltpu.roll(v, 1, 0)

        conduct = rough_ref / rough
        inner = face_s = None
        if mask_rows is not None:
            inner, face_s = mask_rows
            conduct = jnp.where(inner, conduct, 0.0)
        weight_e = jnp.where(face_e, (0.5 * courant) * (conduct + right(conduct)), 0.0)
        weight_s = (0.5 * courant) * (conduct + below(conduct))
        if face_s is not None:
            weight_s = jnp.where(face_s, weight_s, 0.0)

        def advance(v, de, ds):
            flow_e = weight_e * de
            flow_s = weight_s * ds
            return v + ((flow_e - from_left(flow_e)) + (flow_s - from_above(flow_s)))

        for s in range(STEPS):
            de = right(depth) - depth
            ds = below(depth) - depth
            diff_e[s, pl.ds(0, deep)] = de
            diff_s[s, pl.ds(0, deep)] = ds
            if s < STEPS - 1:
                depth = advance(depth, de, ds)
        prod_e = jnp.zeros((deep, cols), F32)
        prod_s = jnp.zeros((deep, cols), F32)
        for s in reversed(range(STEPS)):
            de = right(adjoint) - adjoint
            ds = below(adjoint) - adjoint
            prod_e = prod_e + diff_e[s, pl.ds(0, deep)] * de
            prod_s = prod_s + diff_s[s, pl.ds(0, deep)] * ds
            adjoint = advance(adjoint, de, ds)
        prod_e = jnp.where(face_e, prod_e, 0.0)
        if face_s is not None:
            prod_s = jnp.where(face_s, prod_s, 0.0)
        product = (prod_e + from_left(prod_e)) + (prod_s + from_above(prod_s))
        gradient = (0.5 * courant) * conduct * product
        square = gradient * gradient
        parts = []
        for value in (gradient, square):
            high = value.astype(BF16).astype(F32)
            parts += [high, value - high]
        return parts, adjoint

    def interior():
        parts, adjoint = sweep(*(ext[f, pl.ds(HALO, rows)] for f in range(3)), None)
        for index, value in enumerate(parts):
            pieces[index] = value
        adj_f[...] = adjoint

    def edges():
        @pl.when(t < nt - 1)
        def _():
            for f in range(3):
                down_copy(f).wait_send()
                up_copy(f).wait_recv()

        @pl.when(t > 0)
        def _():
            for f in range(3):
                up_copy(f).wait_send()
                down_copy(f).wait_recv()

        @pl.when(t == 0)
        def _():
            for f in range(3):
                ext[f, pl.ds(0, HALO)] = jnp.ones((HALO, cols), F32)

        @pl.when(t == nt - 1)
        def _():
            for f in range(3):
                ext[f, pl.ds(HALO + rows, HALO)] = jnp.ones((HALO, cols), F32)

        strip = 2 * HALO
        local = iota((2 * strip, cols), 0)
        row_id = jnp.where(local < strip, local, local + (rows - strip))
        first = jnp.where(t == 0, HALO, 0)
        last = jnp.where(t == nt - 1, HALO + rows - 1, rows + 2 * HALO - 1)
        masks = (
            (row_id >= first) & (row_id <= last), (row_id >= first) & (row_id < last)
        )
        parts, adjoint = sweep(
            *(
                jnp.concatenate([ext[f, pl.ds(0, strip)], ext[f, pl.ds(rows, strip)]], axis=0)
                for f in range(3)
            ),
            masks,
        )
        low = strip + HALO - STEPS
        for index, value in enumerate(parts):
            pieces[index, pl.ds(0, STEPS)] = value[HALO : HALO + STEPS]
            pieces[index, pl.ds(rows - STEPS, STEPS)] = value[low : low + STEPS]
        adj_f[pl.ds(0, STEPS)] = adjoint[HALO : HALO + STEPS]
        adj_f[pl.ds(rows - STEPS, STEPS)] = adjoint[low : low + STEPS]
    for load in loads[:3]:
        load.wait()
    interior()
    loads[3].wait()
    owner = owner_in[...].astype(F32)
    device = jnp.floor((owner + 0.5) * (1.0 / span))
    inside = owner - device * span
    block = jnp.floor(inside * (1.0 / LANES))
    group = device * gp + block
    lane = inside - block * LANES
    owner_f[...] = jnp.zeros(owner_f.shape, F32)
    held = owner.shape[0]
    parts = [lane]
    for digit in range(digits):
        upper = jnp.floor(group * (1.0 / 256.0))
        parts.append((group - upper * 256.0) * float(LANES * 256**digit))
        group = upper
    for index, value in enumerate(parts):
        owner_f[pl.ds(0, held)] = value
        table[:, pl.ds(index * label_groups, label_groups)] = owner_f[...].T.astype(BF16)
    count = iota((256, LANES), 0).astype(F32).astype(BF16)

    def spread_rows(row, size):
        tall = jnp.broadcast_to(row, (16, LANES)).astype(BF16)
        return jnp.concatenate([tall] * (size // 16), axis=0)

    def row_of(ref, row):
        return ref[pl.ds(row, 1), :]

    def hot_rows(size, index):
        if size > 256:
            return jnp.where(iota((size, cols), 0) == index, 1.0, 0.0).astype(BF16)
        narrow = index.astype(F32)
        return jnp.concatenate(
            [
                jnp.where(
                    count[:size] == spread_rows(narrow[:, c : c + LANES], size), BF16(1), BF16(0)
                )
                for c in range(0, cols, LANES)
            ],
            axis=1,
        )

    def look_up(chunk, unused):
        for q in range(ROWS_AT_ONCE):
            row = chunk * ROWS_AT_ONCE + q
            labels = row_of(label_in, row)
            hot = hot_rows(label_groups, lax.shift_right_logical(labels, 7))
            found = jnp.dot(
                table[...],
                jnp.concatenate([hot] * (1 + digits), axis=0),
                preferred_element_type=F32,
            )
            mask = iota((LANES, cols), 0) == jnp.bitwise_and(labels, LANES - 1)
            slot_s[pl.ds(row, 1), :] = jnp.sum(
                jnp.where(mask, found, 0.0), axis=0, keepdims=True
            )
        return unused

    loads[4].wait()
    chunks = rows // ROWS_AT_ONCE
    lax.fori_loop(0, chunks, look_up, 0)
    pl.semaphore_wait(barrier, blocks - 1 + len(near))
    start_halos()
    for load in loads[5:]:
        load.wait()

    def gather_rows(row_of_chunk, chunk, unused):
        hot_groups = []
        weighted = []
        for q in range(ROWS_AT_ONCE):
            row = row_of_chunk(chunk, q)
            slot = row_of(slot_s, row).astype(I32)
            hot_groups.append(hot_rows(groups, lax.shift_right_logical(slot, 7)))
            lane_row = jnp.bitwise_and(slot, LANES - 1).astype(F32)
            values = [pieces[i, pl.ds(row, 1), :] for i in range(4)]
            masked = []
            for c in range(0, cols, LANES):
                mask = count[:LANES] == spread_rows(lane_row[:, c : c + LANES], LANES)
                masked.append(
                    jnp.concatenate(
                        [
                            jnp.where(mask, spread_rows(v[:, c : c + LANES], LANES), BF16(0))
                            for v in values
                        ],
                        axis=0,
                    )
                )
            weighted.append(jnp.concatenate(masked, axis=1))
        hist[...] += nt_dot(
            jnp.concatenate(weighted, axis=1), jnp.concatenate(hot_groups, axis=1)
        )
        return unused

    def pair_copy():
        return pltpu.make_async_remote_copy(
            src_ref=sums.at[1 - side],
            dst_ref=pair,
            send_sem=one_send,
            recv_sem=one_recv,
            device_id=(b, t + 1 - 2 * side),
            device_id_type=MESH,
        )

    def two_copy(k):
        other, device = peer(k)
        return pltpu.make_async_remote_copy(
            src_ref=part.at[other],
            dst_ref=recv2.at[k - 1],
            send_sem=two_send.at[k - 1],
            recv_sem=two_recv.at[k - 1],
            device_id=device,
            device_id_type=MESH,
        )

    hist[...] = jnp.zeros(hist.shape, F32)
    half = ROWS_AT_ONCE // 2
    lax.fori_loop(
        0, chunks - 1,
        functools.partial(gather_rows, lambda chunk, q: half + chunk * ROWS_AT_ONCE + q), 0,
    )
    edges()
    gather_rows(lambda chunk, q: q if q < half else rows - ROWS_AT_ONCE + q, 0, 0)
    for which in range(2):
        low = 2 * which * LANES
        total = (hist[pl.ds(low, LANES)] + hist[pl.ds(low + LANES, LANES)]).T
        total = total.reshape(blocks, 2, gp, LANES)
        for p in range(2):
            sums[p, :, which] = total[:, p]
    pair_copy().start()
    rest = adj_f[...]
    for piece in range(3):
        high = rest.astype(BF16)
        adj0[pl.ds(piece * rows, rows)] = high
        rest = rest - high.astype(F32)
    pair_copy().wait()
    part[...] = sums[side] + pair[...]
    for k in range(1, blocks):
        two_copy(k).start()
    reaches, chains = cell_in.shape
    shift = cols.bit_length() - 1

    def levees(chunk, unused):
        base = chunk * 4
        cells = jnp.concatenate([row_of(cell_in, base + q) for q in range(4)], axis=1)
        wide = 4 * chains
        column = jnp.bitwise_and(cells, cols - 1)
        line = lax.shift_right_logical(cells, shift)
        hot = jnp.where(iota((cols, wide), 0) == column, 1.0, 0.0).astype(BF16)
        picked = jnp.dot(adj0[...], hot, preferred_element_type=F32)
        picked = (picked[:rows] + picked[rows : 2 * rows]) + picked[2 * rows :]
        value = jnp.sum(
            jnp.where(iota((rows, wide), 0) == line, picked, 0.0), axis=0, keepdims=True
        )
        for q in range(4):
            levee[pl.ds(base + q, 1), :] = value[:, q * chains : (q + 1) * chains]
        return unused

    lax.fori_loop(0, reaches // 4, levees, 0)

    rate = keep_in[...]
    push = force_in[...] + levee_gain * levee[...]
    reach_id = iota((reaches, chains), 0)
    step = 1
    while step < reaches:
        has = reach_id < reaches - step
        next_rate = jnp.where(has, pltpu.roll(rate, reaches - step, 0), 1.0)
        next_push = jnp.where(has, pltpu.roll(push, reaches - step, 0), 0.0)
        push = push + rate * next_push
        rate = rate * next_rate
        step *= 2
    maps[0, pl.ds(0, 1)] = rate[0:1]
    maps[0, pl.ds(1, 1)] = push[0:1]
    maps[0, pl.ds(2, 6)] = jnp.zeros((6, chains), F32)

    def map_copy(k):
        return pltpu.make_async_remote_copy(
            src_ref=maps.at[0],
            dst_ref=maps.at[k],
            send_sem=map_send.at[k - 1],
            recv_sem=map_recv.at[k - 1],
            device_id=(lax.rem(b + k, nb), t),
            device_id_type=MESH,
        )

    for k in range(1, nb):
        map_copy(k).start()

    for k in range(1, nb):
        map_copy(k).wait()
    incoming = jnp.zeros((1, chains), F32)
    for other in reversed(range(nb)):
        slot = lax.rem(b - other + nb, nb)
        stretch = maps[slot]
        incoming = jnp.where(
            other > b, stretch[0:1] * incoming + stretch[1:2], incoming
        )
    packed_out[pl.ds(2 * gp, reaches)] = rate * incoming + push
    for k in range(1, blocks):
        two_copy(k).wait()
    total = part[mine]
    for k in range(1, blocks):
        total = total + recv2[k - 1]
    for which in range(2):
        packed_out[pl.ds(which * gp, gp)] = total[which]


def unpack(gp, packed_in, grad_out, curv_out, reach_out):
    grad_out[...] = packed_in[pl.ds(0, gp)]
    curv_out[...] = packed_in[pl.ds(gp, gp)]
    reach_out[...] = packed_in[pl.ds(2 * gp, reach_out.shape[0])]


def per_device(
    nb, nt, depth_start, roughness, depth_seed, zone_label, owner_slot, retention, forcing,
    levee_cell,
):
    zones = owner_slot.shape[0]
    span = zones // (nb * nt)
    gp = round_up(round_up(span, LANES) // LANES, 8)
    groups = nb * nt * gp
    digits = 1 if groups <= 256 else 2
    blocks = nb * nt // 2
    rows, cols = depth_start.shape[1:]
    reaches, chains = retention.shape
    padded = round_up(zones, LANES)
    owner = jnp.pad(owner_slot, (0, padded - zones)).reshape(-1, LANES)
    label_groups = round_up(owner.shape[0], LANES)
    deep = rows + 2 * HALO
    vmem = pl.BlockSpec(memory_space=pltpu.VMEM)
    dma = pltpu.SemaphoreType.DMA
    packed = pl.pallas_call(
        functools.partial(kernel, nb, nt, span, gp, digits),
        out_shape=jax.ShapeDtypeStruct((2 * gp + reaches, LANES), F32),
        in_specs=[pl.BlockSpec(memory_space=pl.ANY)] * 8,
        out_specs=vmem,
        scratch_shapes=[
            pltpu.VMEM((rows, cols), I32),
            pltpu.VMEM(owner.shape, I32),
            pltpu.VMEM((reaches, chains), F32),
            pltpu.VMEM((reaches, chains), F32),
            pltpu.VMEM((reaches, chains), I32),
            pltpu.VMEM((3, deep, cols), F32),
            pltpu.VMEM((LANES, (1 + digits) * label_groups), BF16),
            pltpu.VMEM((label_groups, LANES), F32),
            pltpu.VMEM((rows, cols), F32),
            pltpu.VMEM((4, rows, cols), F32),
            pltpu.VMEM((STEPS, rows, cols), F32),
            pltpu.VMEM((STEPS, rows, cols), F32),
            pltpu.VMEM((rows, cols), F32),
            pltpu.VMEM((3 * rows, cols), BF16),
            pltpu.VMEM((reaches, chains), F32),
            pltpu.VMEM((4 * LANES, groups), F32),
            pltpu.VMEM((2, blocks, 2, gp, LANES), F32),
            pltpu.VMEM((blocks, 2, gp, LANES), F32),
            pltpu.VMEM((blocks, 2, gp, LANES), F32),
            pltpu.VMEM((blocks - 1, 2, gp, LANES), F32),
            pltpu.VMEM((nb, 8, chains), F32),
            dma((2, 3)), dma((2, 3)),
            dma((nb - 1,)), dma((nb - 1,)),
            dma, dma,
            dma((blocks - 1,)), dma((blocks - 1,)),
            dma((8,)),
        ],
        compiler_params=pltpu.CompilerParams(collective_id=0, has_side_effects=True),
    )(
        depth_start[0], roughness[0], depth_seed[0], zone_label[0], owner, retention, forcing,
        levee_cell,
    )
    grad, curv, reach = pl.pallas_call(
        functools.partial(unpack, gp),
        out_shape=(
            jax.ShapeDtypeStruct((gp, LANES), F32),
            jax.ShapeDtypeStruct((gp, LANES), F32),
            jax.ShapeDtypeStruct((reaches, chains), F32),
        ),
        in_specs=[vmem],
        out_specs=(vmem,) * 3,
    )(packed)
    return grad.reshape(-1)[:span], curv.reshape(-1)[:span], reach


def solution(mesh):
    in_specs = (
        P("basin", "tile", None),
        P("basin", "tile", None),
        P("basin", "tile", None),
        P("basin", "tile", None),
        P(),
        P("basin", "tile"),
        P("basin", "tile"),
        P("basin", "tile"),
    )
    out_specs = (P(("basin", "tile")), P(("basin", "tile")), P("basin", "tile"))
    return jax.shard_map(
        functools.partial(per_device, mesh.shape["basin"], mesh.shape["tile"]),
        mesh=mesh, in_specs=in_specs, out_specs=out_specs, check_vma=False,
    )
```

```python
import functools

import jax
import jax.numpy as jnp
from jax import lax
from jax.experimental import pallas as pl
from jax.experimental.pallas import tpu as pltpu
from jax.sharding import PartitionSpec as P

STEPS = 4
HALO = 8
LANES = 128
ROWS_AT_ONCE = 8

courant = 0.24
rough_ref = 0.025
levee_gain = 0.1

F32 = jnp.float32
BF16 = jnp.bfloat16
I32 = jnp.int32
MESH = pl.DeviceIdType.MESH


def round_up(value, unit):
    return -(-value // unit) * unit


def iota(shape, dim):
    return lax.broadcasted_iota(I32, shape, dim)


def nt_dot(left, right):
    return lax.dot_general(
        left, right, (((1,), (1,)), ((), ())), preferred_element_type=F32
    )


def main_kernel(
    nb, nt, span, gp, digits, window,
    depth_in, rough_in, seed_in, label_hbm, owner_hbm, keep_hbm, force_hbm, cell_hbm,
    packed_out,
    label_in, owner_in, keep_in, force_in, cell_in, ext, table, owner_f, slot_tab, cells, pieces, packed, home_sums, home_parts, diff_e, diff_s, adj_f,
    adj0, levee, hist, sums, pair, part, recv2, maps,
    halo_send, halo_recv, map_send, map_recv, one_send, one_recv, two_send, two_recv, load_sem,
):
    b = lax.axis_index("basin")
    t = lax.axis_index("tile")
    rows, cols = depth_in.shape
    label_groups = table.shape[1] // (1 + digits)
    groups = nb * nt * gp

    blocks = nb * nt // 2
    side = lax.rem(t, 2)
    mine = b * (nt // 2) + t // 2

    def peer(k):
        other = lax.rem(mine + k, blocks)
        return other, (other // (nt // 2), 2 * lax.rem(other, nt // 2) + side)

    barrier = pltpu.get_barrier_semaphore()
    for k in range(1, blocks):
        pl.semaphore_signal(barrier, inc=1, device_id=peer(k)[1], device_id_type=MESH)
    near = sorted({1, nt - 1})
    for k in near:
        pl.semaphore_signal(
            barrier, inc=1, device_id=(b, lax.rem(t + k, nt)), device_id_type=MESH
        )

    fields = (depth_in, rough_in, seed_in)
    pairs = (
        (depth_in, ext.at[0, pl.ds(HALO, rows)]), (rough_in, ext.at[1, pl.ds(HALO, rows)]),
        (seed_in, ext.at[2, pl.ds(HALO, rows)]),
        (owner_hbm, owner_in), (label_hbm, label_in),
        (cell_hbm, cell_in), (keep_hbm, keep_in), (force_hbm, force_in),
    )
    loads = [
        pltpu.make_async_copy(source, target, load_sem.at[index])
        for index, (source, target) in enumerate(pairs)
    ]
    for load in loads:
        load.start()

    def down_copy(f):
        return pltpu.make_async_remote_copy(
            src_ref=fields[f].at[pl.ds(rows - HALO, HALO)],
            dst_ref=ext.at[f, pl.ds(0, HALO)],
            send_sem=halo_send.at[0, f],
            recv_sem=halo_recv.at[0, f],
            device_id=(b, lax.rem(t + 1, nt)),
            device_id_type=MESH,
        )

    def up_copy(f):
        return pltpu.make_async_remote_copy(
            src_ref=fields[f].at[pl.ds(0, HALO)],
            dst_ref=ext.at[f, pl.ds(HALO + rows, HALO)],
            send_sem=halo_send.at[1, f],
            recv_sem=halo_recv.at[1, f],
            device_id=(b, lax.rem(t + nt - 1, nt)),
            device_id_type=MESH,
        )

    def start_halos():
        @pl.when(t < nt - 1)
        def _():
            for f in range(3):
                down_copy(f).start()

        @pl.when(t > 0)
        def _():
            for f in range(3):
                up_copy(f).start()

    def right(v):
        return pltpu.roll(v, cols - 1, 1)

    def from_left(v):
        return pltpu.roll(v, 1, 1)

    def sweep(depth, rough, adjoint, mask_rows):
        deep = depth.shape[0]
        face_e = iota((deep, cols), 1) < cols - 1

        def below(v):
            return pltpu.roll(v, deep - 1, 0)

        def from_above(v):
            return pltpu.roll(v, 1, 0)

        conduct = rough_ref / rough
        inner = face_s = None
        if mask_rows is not None:
            inner, face_s = mask_rows
            conduct = jnp.where(inner, conduct, 0.0)
        weight_e = jnp.where(face_e, (0.5 * courant) * (conduct + right(conduct)), 0.0)
        weight_s = (0.5 * courant) * (conduct + below(conduct))
        if face_s is not None:
            weight_s = jnp.where(face_s, weight_s, 0.0)

        def advance(v, de, ds):
            flow_e = weight_e * de
            flow_s = weight_s * ds
            return v + ((flow_e - from_left(flow_e)) + (flow_s - from_above(flow_s)))

        for s in range(STEPS):
            de = right(depth) - depth
            ds = below(depth) - depth
            diff_e[s, pl.ds(0, deep)] = de
            diff_s[s, pl.ds(0, deep)] = ds
            if s < STEPS - 1:
                depth = advance(depth, de, ds)
        prod_e = jnp.zeros((deep, cols), F32)
        prod_s = jnp.zeros((deep, cols), F32)
        for s in reversed(range(STEPS)):
            de = right(adjoint) - adjoint
            ds = below(adjoint) - adjoint
            prod_e = prod_e + diff_e[s, pl.ds(0, deep)] * de
            prod_s = prod_s + diff_s[s, pl.ds(0, deep)] * ds
            adjoint = advance(adjoint, de, ds)
        prod_e = jnp.where(face_e, prod_e, 0.0)
        if face_s is not None:
            prod_s = jnp.where(face_s, prod_s, 0.0)
        product = (prod_e + from_left(prod_e)) + (prod_s + from_above(prod_s))
        gradient = (0.5 * courant) * conduct * product
        square = gradient * gradient
        parts = []
        for value in (gradient, square):
            high = value.astype(BF16).astype(F32)
            parts += [high, value - high]
        return parts, adjoint

    def interior():
        parts, adjoint = sweep(*(ext[f, pl.ds(HALO, rows)] for f in range(3)), None)
        for index, value in enumerate(parts):
            pieces[index] = value
        adj_f[...] = adjoint

    def edges():
        @pl.when(t < nt - 1)
        def _():
            for f in range(3):
                down_copy(f).wait_send()
                up_copy(f).wait_recv()

        @pl.when(t > 0)
        def _():
            for f in range(3):
                up_copy(f).wait_send()
                down_copy(f).wait_recv()

        @pl.when(t == 0)
        def _():
            for f in range(3):
                ext[f, pl.ds(0, HALO)] = jnp.ones((HALO, cols), F32)

        @pl.when(t == nt - 1)
        def _():
            for f in range(3):
                ext[f, pl.ds(HALO + rows, HALO)] = jnp.ones((HALO, cols), F32)

        strip = 2 * HALO
        local = iota((2 * strip, cols), 0)
        row_id = jnp.where(local < strip, local, local + (rows - strip))
        first = jnp.where(t == 0, HALO, 0)
        last = jnp.where(t == nt - 1, HALO + rows - 1, rows + 2 * HALO - 1)
        masks = (
            (row_id >= first) & (row_id <= last), (row_id >= first) & (row_id < last)
        )
        parts, adjoint = sweep(
            *(
                jnp.concatenate([ext[f, pl.ds(0, strip)], ext[f, pl.ds(rows, strip)]], axis=0)
                for f in range(3)
            ),
            masks,
        )
        low = strip + HALO - STEPS
        for index, value in enumerate(parts):
            pieces[index, pl.ds(0, STEPS)] = value[HALO : HALO + STEPS]
            pieces[index, pl.ds(rows - STEPS, STEPS)] = value[low : low + STEPS]
        adj_f[pl.ds(0, STEPS)] = adjoint[HALO : HALO + STEPS]
        adj_f[pl.ds(rows - STEPS, STEPS)] = adjoint[low : low + STEPS]
    for load in loads[:3]:
        load.wait()
    interior()
    loads[3].wait()
    owner = owner_in[...].astype(F32)
    device = jnp.floor((owner + 0.5) * (1.0 / span))
    inside = owner - device * span
    block = jnp.floor(inside * (1.0 / LANES))
    group = device * gp + block
    lane = inside - block * LANES
    owner_f[...] = jnp.zeros(owner_f.shape, F32)
    slot_tab[...] = jnp.zeros(slot_tab.shape, F32)
    held = owner.shape[0]
    slot_tab[pl.ds(0, held)] = group * LANES + lane
    parts = [lane]
    for digit in range(digits):
        upper = jnp.floor(group * (1.0 / 256.0))
        parts.append((group - upper * 256.0) * float(LANES * 256**digit))
        group = upper
    for index, value in enumerate(parts):
        owner_f[pl.ds(0, held)] = value
        table[:, pl.ds(index * label_groups, label_groups)] = owner_f[...].T.astype(BF16)
    count = iota((256, LANES), 0).astype(F32).astype(BF16)

    def spread_rows(row, size):
        tall = jnp.broadcast_to(row, (16, LANES)).astype(BF16)
        return tall if size == 16 else jnp.concatenate([tall] * (size // 16), axis=0)

    def row_of(ref, row):
        return ref[pl.ds(row, 1), :]

    def hot_rows(size, index):
        if size > 256:
            return jnp.where(iota((size, LANES), 0) == index.astype(I32), 1.0, 0.0).astype(BF16)
        return jnp.where(count[:size] == spread_rows(index, size), BF16(1), BF16(0))

    def side_by_side(pieces_of_row):
        return jnp.concatenate(pieces_of_row, axis=1)

    dev = b * nt + t
    first_group = (dev * span) // LANES
    home_rows = round_up(window, 16)

    def prepare():
        labels = label_in[...]
        group_of = lax.shift_right_logical(labels, 7)
        place = group_of - first_group
        stray = (place < 0) | (place >= window)
        before = jnp.where(iota((cols, cols), 0) <= iota((cols, cols), 1), 1.0, 0.0).astype(BF16)
        rank = jnp.dot(
            jnp.where(stray, 1.0, 0.0).astype(BF16), before, preferred_element_type=F32
        )
        cells[0] = group_of.astype(F32)
        cells[1] = jnp.bitwise_and(labels, LANES - 1).astype(F32)
        cells[2] = jnp.where(stray, -1.0, place.astype(F32))
        cells[3] = jnp.where(stray, rank - 1.0, -1.0)
        most = jnp.max(jnp.max(rank, axis=0, keepdims=True), axis=1, keepdims=True)
        over = jnp.where(most > LANES, 1.0, 0.0)
        hist[...] = jnp.zeros(hist.shape, F32)
        hist[pl.ds(LANES - 1, 1)] = jnp.where(
            lax.rem(iota((1, groups), 1), gp) == gp - 1, over, 0.0
        )
        home_sums[...] = jnp.zeros(home_sums.shape, F32)

    def compact(rows_of_chunk):
        line = count[:16]
        total = None
        for q, row in enumerate(rows_of_chunk):
            left, right_side = [], []
            labels = [cells[i, pl.ds(row, 1), :] for i in range(4)]
            amounts = [pieces[i, pl.ds(row, 1), :] for i in range(4)]
            for c in range(0, cols, LANES):
                upper, lower, place, position = (v[:, c : c + LANES] for v in labels)
                values = [spread_rows(v[:, c : c + LANES], 16) for v in amounts]
                right_side.append(
                    jnp.concatenate([hot_rows(LANES, position), hot_rows(LANES, lower)], axis=0)
                )
                carried = BF16(0)
                for i, value in enumerate([spread_rows(upper, 16), spread_rows(lower, 16)] + values):
                    carried = jnp.where(line == BF16(i), value, carried)
                weighted = []
                for first_row in range(0, home_rows, 16):
                    mask = count[first_row : first_row + 16] == spread_rows(place, 16)
                    weighted.append([jnp.where(mask, value, BF16(0)) for value in values])
                left.append(
                    jnp.concatenate(
                        [carried] + [part_of[i] for i in range(4) for part_of in weighted], axis=0
                    )
                )
            found = nt_dot(side_by_side(left), side_by_side(right_side))
            packed[pl.ds(8 * q, 8)] = found[:8, :LANES]
            homes = found[16:, LANES:]
            total = homes if total is None else total + homes
        home_sums[...] += total

    def add_to_slots(slots, values_of):
        hot_groups = []
        weighted = []
        for slot, values in zip(slots, values_of):
            index = slot.astype(I32)
            hot_groups.append(hot_rows(groups, lax.shift_right_logical(index, 7).astype(F32)))
            lane_row = jnp.bitwise_and(index, LANES - 1).astype(F32)
            mask = count[:LANES] == spread_rows(lane_row, LANES)
            weighted.append(
                jnp.concatenate(
                    [jnp.where(mask, spread_rows(v, LANES), BF16(0)) for v in values], axis=0
                )
            )
        hist[...] += nt_dot(side_by_side(weighted), side_by_side(hot_groups))

    def scatter_strays():
        hot = side_by_side(
            [hot_rows(label_groups, row_of(packed, 8 * q)) for q in range(ROWS_AT_ONCE)]
        )
        found = jnp.dot(
            table[...], jnp.concatenate([hot] * (1 + digits), axis=0), preferred_element_type=F32
        )
        slots = []
        for q in range(ROWS_AT_ONCE):
            mask = iota((LANES, LANES), 0) == row_of(packed, 8 * q + 1).astype(I32)
            slots.append(
                jnp.sum(
                    jnp.where(mask, found[:, q * LANES : (q + 1) * LANES], 0.0),
                    axis=0, keepdims=True,
                )
            )
        add_to_slots(
            slots,
            [[row_of(packed, 8 * q + 2 + i) for i in range(4)] for q in range(ROWS_AT_ONCE)],
        )

    def scatter_homes():
        for which in range(2):
            low = 2 * which * home_rows
            value = home_sums[pl.ds(low, home_rows)] + home_sums[pl.ds(low + home_rows, home_rows)]
            high = value.astype(BF16).astype(F32)
            home_parts[2 * which] = high
            home_parts[2 * which + 1] = value - high
        add_to_slots(
            [row_of(slot_tab, first_group + i) for i in range(window)],
            [[home_parts[k, pl.ds(i, 1), :] for k in range(4)] for i in range(window)],
        )

    loads[4].wait()
    chunks = rows // ROWS_AT_ONCE
    half = ROWS_AT_ONCE // 2

    def inner_chunk(chunk, unused):
        compact([half + chunk * ROWS_AT_ONCE + q for q in range(ROWS_AT_ONCE)])
        scatter_strays()
        return unused

    prepare()
    early = (chunks - 1) // 2
    lax.fori_loop(0, early, inner_chunk, 0)
    pl.semaphore_wait(barrier, blocks - 1 + len(near))
    start_halos()
    lax.fori_loop(early, chunks - 1, inner_chunk, 0)
    for load in loads[5:]:
        load.wait()

    def pair_copy():
        return pltpu.make_async_remote_copy(
            src_ref=sums.at[1 - side],
            dst_ref=pair,
            send_sem=one_send,
            recv_sem=one_recv,
            device_id=(b, t + 1 - 2 * side),
            device_id_type=MESH,
        )

    def two_copy(k):
        other, device = peer(k)
        return pltpu.make_async_remote_copy(
            src_ref=part.at[other],
            dst_ref=recv2.at[k - 1],
            send_sem=two_send.at[k - 1],
            recv_sem=two_recv.at[k - 1],
            device_id=device,
            device_id_type=MESH,
        )

    edges()
    compact([q if q < half else rows - ROWS_AT_ONCE + q for q in range(ROWS_AT_ONCE)])
    scatter_strays()
    scatter_homes()
    for which in range(2):
        low = 2 * which * LANES
        total = (hist[pl.ds(low, LANES)] + hist[pl.ds(low + LANES, LANES)]).T
        total = total.reshape(blocks, 2, gp, LANES)
        for p in range(2):
            sums[p, :, which] = total[:, p]
    pair_copy().start()
    rest = adj_f[...]
    for piece in range(3):
        high = rest.astype(BF16)
        adj0[pl.ds(piece * rows, rows)] = high
        rest = rest - high.astype(F32)
    pair_copy().wait()
    part[...] = sums[side] + pair[...]
    for k in range(1, blocks):
        two_copy(k).start()
    reaches, chains = cell_in.shape
    shift = cols.bit_length() - 1

    def levees(chunk, unused):
        base = chunk * 4
        cells = jnp.concatenate([row_of(cell_in, base + q) for q in range(4)], axis=1)
        wide = 4 * chains
        column = jnp.bitwise_and(cells, cols - 1)
        line = lax.shift_right_logical(cells, shift)
        hot = jnp.where(iota((cols, wide), 0) == column, 1.0, 0.0).astype(BF16)
        picked = jnp.dot(adj0[...], hot, preferred_element_type=F32)
        picked = (picked[:rows] + picked[rows : 2 * rows]) + picked[2 * rows :]
        value = jnp.sum(
            jnp.where(iota((rows, wide), 0) == line, picked, 0.0), axis=0, keepdims=True
        )
        for q in range(4):
            levee[pl.ds(base + q, 1), :] = value[:, q * chains : (q + 1) * chains]
        return unused

    lax.fori_loop(0, reaches // 4, levees, 0)

    rate = keep_in[...]
    push = force_in[...] + levee_gain * levee[...]
    reach_id = iota((reaches, chains), 0)
    step = 1
    while step < reaches:
        has = reach_id < reaches - step
        next_rate = jnp.where(has, pltpu.roll(rate, reaches - step, 0), 1.0)
        next_push = jnp.where(has, pltpu.roll(push, reaches - step, 0), 0.0)
        push = push + rate * next_push
        rate = rate * next_rate
        step *= 2
    maps[0, pl.ds(0, 1)] = rate[0:1]
    maps[0, pl.ds(1, 1)] = push[0:1]
    maps[0, pl.ds(2, 6)] = jnp.zeros((6, chains), F32)

    def map_copy(k):
        return pltpu.make_async_remote_copy(
            src_ref=maps.at[0],
            dst_ref=maps.at[k],
            send_sem=map_send.at[k - 1],
            recv_sem=map_recv.at[k - 1],
            device_id=(lax.rem(b + k, nb), t),
            device_id_type=MESH,
        )

    for k in range(1, nb):
        map_copy(k).start()

    for k in range(1, nb):
        map_copy(k).wait()
    incoming = jnp.zeros((1, chains), F32)
    for other in reversed(range(nb)):
        slot = lax.rem(b - other + nb, nb)
        stretch = maps[slot]
        incoming = jnp.where(
            other > b, stretch[0:1] * incoming + stretch[1:2], incoming
        )
    packed_out[pl.ds(2 * gp, reaches)] = rate * incoming + push
    for k in range(1, blocks):
        two_copy(k).wait()
    total = part[mine]
    for k in range(1, blocks):
        total = total + recv2[k - 1]
    for which in range(2):
        packed_out[pl.ds(which * gp, gp)] = total[which]


def full_kernel(
    nb, nt, span, gp, digits,
    depth_in, rough_in, seed_in, label_hbm, owner_hbm, keep_hbm, force_hbm, cell_hbm,
    packed_out,
    label_in, owner_in, keep_in, force_in, cell_in, ext, table, owner_f, slot_s, pieces, diff_e, diff_s, adj0, levee,
    hist, sums, recv1, part, recv2, maps,
    halo_send, halo_recv, map_send, map_recv, one_send, one_recv, two_send, two_recv, load_sem,
):
    b = lax.axis_index("basin")
    t = lax.axis_index("tile")
    rows, cols = depth_in.shape
    label_groups = table.shape[1] // (1 + digits)
    groups = nb * nt * gp

    barrier = pltpu.get_barrier_semaphore()
    for k in range(1, nb):
        pl.semaphore_signal(
            barrier, inc=1, device_id=(lax.rem(b + k, nb), t), device_id_type=MESH
        )
    for k in range(1, nt):
        pl.semaphore_signal(
            barrier, inc=1, device_id=(b, lax.rem(t + k, nt)), device_id_type=MESH
        )

    fields = (depth_in, rough_in, seed_in)
    pairs = (
        (owner_hbm, owner_in), (label_hbm, label_in),
        (depth_in, ext.at[0, pl.ds(HALO, rows)]), (rough_in, ext.at[1, pl.ds(HALO, rows)]),
        (seed_in, ext.at[2, pl.ds(HALO, rows)]),
        (cell_hbm, cell_in), (keep_hbm, keep_in), (force_hbm, force_in),
    )
    loads = [
        pltpu.make_async_copy(source, target, load_sem.at[index])
        for index, (source, target) in enumerate(pairs)
    ]
    for load in loads:
        load.start()
    pl.semaphore_wait(barrier, nb - 1 + nt - 1)

    def down_copy(f):
        return pltpu.make_async_remote_copy(
            src_ref=fields[f].at[pl.ds(rows - HALO, HALO)],
            dst_ref=ext.at[f, pl.ds(0, HALO)],
            send_sem=halo_send.at[0, f],
            recv_sem=halo_recv.at[0, f],
            device_id=(b, lax.rem(t + 1, nt)),
            device_id_type=MESH,
        )

    def up_copy(f):
        return pltpu.make_async_remote_copy(
            src_ref=fields[f].at[pl.ds(0, HALO)],
            dst_ref=ext.at[f, pl.ds(HALO + rows, HALO)],
            send_sem=halo_send.at[1, f],
            recv_sem=halo_recv.at[1, f],
            device_id=(b, lax.rem(t + nt - 1, nt)),
            device_id_type=MESH,
        )

    @pl.when(t < nt - 1)
    def _():
        for f in range(3):
            down_copy(f).start()

    @pl.when(t > 0)
    def _():
        for f in range(3):
            up_copy(f).start()

    loads[0].wait()
    owner = owner_in[...].astype(F32)
    device = jnp.floor((owner + 0.5) * (1.0 / span))
    inside = owner - device * span
    block = jnp.floor(inside * (1.0 / LANES))
    group = device * gp + block
    lane = inside - block * LANES
    owner_f[...] = jnp.zeros(owner_f.shape, F32)
    held = owner.shape[0]
    parts = [lane]
    for digit in range(digits):
        upper = jnp.floor(group * (1.0 / 256.0))
        parts.append((group - upper * 256.0) * float(LANES * 256**digit))
        group = upper
    for index, value in enumerate(parts):
        owner_f[pl.ds(0, held)] = value
        table[:, pl.ds(index * label_groups, label_groups)] = owner_f[...].T.astype(BF16)
    count = iota((256, LANES), 0).astype(F32).astype(BF16)

    def spread_rows(row, size):
        tall = jnp.broadcast_to(row, (16, LANES)).astype(BF16)
        return jnp.concatenate([tall] * (size // 16), axis=0)

    def row_of(ref, row):
        return ref[pl.ds(row, 1), :]

    def hot_rows(size, index):
        if size > 256:
            return jnp.where(iota((size, cols), 0) == index, 1.0, 0.0).astype(BF16)
        narrow = index.astype(F32)
        return jnp.concatenate(
            [
                jnp.where(
                    count[:size] == spread_rows(narrow[:, c : c + LANES], size), BF16(1), BF16(0)
                )
                for c in range(0, cols, LANES)
            ],
            axis=1,
        )

    def look_up(chunk, unused):
        for q in range(ROWS_AT_ONCE):
            row = chunk * ROWS_AT_ONCE + q
            labels = row_of(label_in, row)
            hot = hot_rows(label_groups, lax.shift_right_logical(labels, 7))
            found = jnp.dot(
                table[...],
                jnp.concatenate([hot] * (1 + digits), axis=0),
                preferred_element_type=F32,
            )
            mask = iota((LANES, cols), 0) == jnp.bitwise_and(labels, LANES - 1)
            slot_s[pl.ds(row, 1), :] = jnp.sum(
                jnp.where(mask, found, 0.0), axis=0, keepdims=True
            )
        return unused

    loads[1].wait()
    lax.fori_loop(0, rows // ROWS_AT_ONCE, look_up, 0)
    for load in loads[2:]:
        load.wait()

    @pl.when(t < nt - 1)
    def _():
        for f in range(3):
            down_copy(f).wait_send()
            up_copy(f).wait_recv()

    @pl.when(t > 0)
    def _():
        for f in range(3):
            up_copy(f).wait_send()
            down_copy(f).wait_recv()

    @pl.when(t == 0)
    def _():
        for f in range(3):
            ext[f, pl.ds(0, HALO)] = jnp.ones((HALO, cols), F32)

    @pl.when(t == nt - 1)
    def _():
        for f in range(3):
            ext[f, pl.ds(HALO + rows, HALO)] = jnp.ones((HALO, cols), F32)

    deep = rows + 2 * HALO
    row_id = iota((deep, cols), 0)
    col_id = iota((deep, cols), 1)
    first = jnp.where(t == 0, HALO, 0)
    last = jnp.where(t == nt - 1, HALO + rows - 1, deep - 1)
    inner = (row_id >= first) & (row_id <= last)
    face_s = (row_id >= first) & (row_id < last)
    face_e = col_id < cols - 1

    def below(v):
        return pltpu.roll(v, deep - 1, 0)

    def right(v):
        return pltpu.roll(v, cols - 1, 1)

    def from_above(v):
        return pltpu.roll(v, 1, 0)

    def from_left(v):
        return pltpu.roll(v, 1, 1)

    conduct = jnp.where(inner, rough_ref / ext[1], 0.0)
    weight_e = jnp.where(face_e, (0.5 * courant) * (conduct + right(conduct)), 0.0)
    weight_s = jnp.where(face_s, (0.5 * courant) * (conduct + below(conduct)), 0.0)

    def advance(v, de, ds):
        flow_e = weight_e * de
        flow_s = weight_s * ds
        return v + ((flow_e - from_left(flow_e)) + (flow_s - from_above(flow_s)))

    depth = ext[0]
    for s in range(STEPS):
        de = right(depth) - depth
        ds = below(depth) - depth
        diff_e[s] = de
        diff_s[s] = ds
        if s < STEPS - 1:
            depth = advance(depth, de, ds)
    adjoint = ext[2]
    prod_e = jnp.zeros((deep, cols), F32)
    prod_s = jnp.zeros((deep, cols), F32)
    for s in reversed(range(STEPS)):
        de = right(adjoint) - adjoint
        ds = below(adjoint) - adjoint
        prod_e = prod_e + diff_e[s] * de
        prod_s = prod_s + diff_s[s] * ds
        adjoint = advance(adjoint, de, ds)
    prod_e = jnp.where(face_e, prod_e, 0.0)
    prod_s = jnp.where(face_s, prod_s, 0.0)
    product = (prod_e + from_left(prod_e)) + (prod_s + from_above(prod_s))
    gradient = ((0.5 * courant) * conduct * product)[HALO : HALO + rows]
    square = gradient * gradient
    for index, value in enumerate((gradient, square)):
        high = value.astype(BF16).astype(F32)
        pieces[2 * index] = high
        pieces[2 * index + 1] = value - high

    def gather_rows(which, chunk, unused):
        hot_groups = []
        weighted = []
        for q in range(ROWS_AT_ONCE):
            row = chunk * ROWS_AT_ONCE + q
            slot = row_of(slot_s, row).astype(I32)
            hot_groups.append(hot_rows(groups, lax.shift_right_logical(slot, 7)))
            lane_row = jnp.bitwise_and(slot, LANES - 1).astype(F32)
            values = [pieces[i, pl.ds(row, 1), :] for i in range(4)]
            masked = []
            for c in range(0, cols, LANES):
                mask = count[:LANES] == spread_rows(lane_row[:, c : c + LANES], LANES)
                masked.append(
                    jnp.concatenate(
                        [
                            jnp.where(mask, spread_rows(v[:, c : c + LANES], LANES), BF16(0))
                            for v in values
                        ],
                        axis=0,
                    )
                )
            weighted.append(jnp.concatenate(masked, axis=1))
        hist[...] += nt_dot(
            jnp.concatenate(weighted, axis=1), jnp.concatenate(hot_groups, axis=1)
        )
        return unused

    chunks = rows // ROWS_AT_ONCE

    def one_copy(which, k):
        other = lax.rem(b + k, nb)
        return pltpu.make_async_remote_copy(
            src_ref=sums.at[which, pl.ds(pl.multiple_of(other * (nt * gp), 8), nt * gp)],
            dst_ref=recv1.at[k - 1, which],
            send_sem=one_send.at[which, k - 1],
            recv_sem=one_recv.at[which, k - 1],
            device_id=(other, t),
            device_id_type=MESH,
        )

    def two_copy(which, k):
        other = lax.rem(t + k, nt)
        return pltpu.make_async_remote_copy(
            src_ref=part.at[which, pl.ds(pl.multiple_of(other * gp, 8), gp)],
            dst_ref=recv2.at[k - 1, which],
            send_sem=two_send.at[which, k - 1],
            recv_sem=two_recv.at[which, k - 1],
            device_id=(b, other),
            device_id_type=MESH,
        )

    def collect(which, start, stop):
        lax.fori_loop(start, stop, functools.partial(gather_rows, which), 0)

    def first_phase(which):
        sums[which] = (hist[pl.ds(2 * which * LANES, LANES)] + hist[pl.ds((2 * which + 1) * LANES, LANES)]).T
        for k in range(1, nb):
            one_copy(which, k).start()

    def second_phase(which):
        for k in range(1, nb):
            one_copy(which, k).wait()
        total = sums[which, pl.ds(pl.multiple_of(b * (nt * gp), 8), nt * gp)]
        for k in range(1, nb):
            total = total + recv1[k - 1, which]
        part[which] = total
        for k in range(1, nt):
            two_copy(which, k).start()

    def finish(which):
        for k in range(1, nt):
            two_copy(which, k).wait()
        total = part[which, pl.ds(pl.multiple_of(t * gp, 8), gp)]
        for k in range(1, nt):
            total = total + recv2[k - 1, which]
        packed_out[pl.ds(which * gp, gp)] = total

    hist[...] = jnp.zeros(hist.shape, F32)
    collect(0, 0, chunks)
    first_phase(0)
    first_phase(1)
    rest = adjoint[HALO : HALO + rows]
    for piece in range(3):
        high = rest.astype(BF16)
        adj0[pl.ds(piece * rows, rows)] = high
        rest = rest - high.astype(F32)
    reaches, chains = cell_in.shape
    shift = cols.bit_length() - 1

    def levees(chunk, unused):
        base = chunk * 4
        cells = jnp.concatenate([row_of(cell_in, base + q) for q in range(4)], axis=1)
        wide = 4 * chains
        column = jnp.bitwise_and(cells, cols - 1)
        line = lax.shift_right_logical(cells, shift)
        hot = jnp.where(iota((cols, wide), 0) == column, 1.0, 0.0).astype(BF16)
        picked = jnp.dot(adj0[...], hot, preferred_element_type=F32)
        picked = (picked[:rows] + picked[rows : 2 * rows]) + picked[2 * rows :]
        value = jnp.sum(
            jnp.where(iota((rows, wide), 0) == line, picked, 0.0), axis=0, keepdims=True
        )
        for q in range(4):
            levee[pl.ds(base + q, 1), :] = value[:, q * chains : (q + 1) * chains]
        return unused

    lax.fori_loop(0, reaches // 4, levees, 0)

    rate = keep_in[...]
    push = force_in[...] + levee_gain * levee[...]
    reach_id = iota((reaches, chains), 0)
    step = 1
    while step < reaches:
        has = reach_id < reaches - step
        next_rate = jnp.where(has, pltpu.roll(rate, reaches - step, 0), 1.0)
        next_push = jnp.where(has, pltpu.roll(push, reaches - step, 0), 0.0)
        push = push + rate * next_push
        rate = rate * next_rate
        step *= 2
    maps[0, pl.ds(0, 1)] = rate[0:1]
    maps[0, pl.ds(1, 1)] = push[0:1]
    maps[0, pl.ds(2, 6)] = jnp.zeros((6, chains), F32)

    def map_copy(k):
        return pltpu.make_async_remote_copy(
            src_ref=maps.at[0],
            dst_ref=maps.at[k],
            send_sem=map_send.at[k - 1],
            recv_sem=map_recv.at[k - 1],
            device_id=(lax.rem(b + k, nb), t),
            device_id_type=MESH,
        )

    for k in range(1, nb):
        map_copy(k).start()

    second_phase(0)
    second_phase(1)
    for k in range(1, nb):
        map_copy(k).wait()
    incoming = jnp.zeros((1, chains), F32)
    for other in reversed(range(nb)):
        slot = lax.rem(b - other + nb, nb)
        stretch = maps[slot]
        incoming = jnp.where(
            other > b, stretch[0:1] * incoming + stretch[1:2], incoming
        )
    packed_out[pl.ds(2 * gp, reaches)] = rate * incoming + push
    finish(0)
    finish(1)


def unpack(gp, packed_in, grad_out, curv_out, reach_out):
    grad_out[...] = packed_in[pl.ds(0, gp)]
    curv_out[...] = packed_in[pl.ds(gp, gp)]
    reach_out[...] = packed_in[pl.ds(2 * gp, reach_out.shape[0])]


def full_pass(
    nb, nt, gp, depth_start, roughness, depth_seed, zone_label, owner_slot, retention, forcing,
    levee_cell,
):
    zones = owner_slot.shape[0]
    span = zones // (nb * nt)
    groups = nb * nt * gp
    digits = 1 if groups <= 256 else 2
    rows, cols = depth_start.shape[1:]
    reaches, chains = retention.shape
    padded = round_up(zones, LANES)
    owner = jnp.pad(owner_slot, (0, padded - zones)).reshape(-1, LANES)
    label_groups = round_up(owner.shape[0], LANES)
    deep = rows + 2 * HALO
    vmem = pl.BlockSpec(memory_space=pltpu.VMEM)
    dma = pltpu.SemaphoreType.DMA
    return pl.pallas_call(
        functools.partial(full_kernel, nb, nt, span, gp, digits),
        out_shape=jax.ShapeDtypeStruct((2 * gp + reaches, LANES), F32),
        in_specs=[pl.BlockSpec(memory_space=pl.ANY)] * 8,
        out_specs=vmem,
        scratch_shapes=[
            pltpu.VMEM((rows, cols), I32),
            pltpu.VMEM(owner.shape, I32),
            pltpu.VMEM((reaches, chains), F32),
            pltpu.VMEM((reaches, chains), F32),
            pltpu.VMEM((reaches, chains), I32),
            pltpu.VMEM((3, deep, cols), F32),
            pltpu.VMEM((LANES, (1 + digits) * label_groups), BF16),
            pltpu.VMEM((label_groups, LANES), F32),
            pltpu.VMEM((rows, cols), F32),
            pltpu.VMEM((4, rows, cols), F32),
            pltpu.VMEM((STEPS, deep, cols), F32),
            pltpu.VMEM((STEPS, deep, cols), F32),
            pltpu.VMEM((3 * rows, cols), BF16),
            pltpu.VMEM((reaches, chains), F32),
            pltpu.VMEM((4 * LANES, groups), F32),
            pltpu.VMEM((2, groups, LANES), F32),
            pltpu.VMEM((nb - 1, 2, nt * gp, LANES), F32),
            pltpu.VMEM((2, nt * gp, LANES), F32),
            pltpu.VMEM((nt - 1, 2, gp, LANES), F32),
            pltpu.VMEM((nb, 8, chains), F32),
            dma((2, 3)), dma((2, 3)),
            dma((nb - 1,)), dma((nb - 1,)),
            dma((2, nb - 1)), dma((2, nb - 1)),
            dma((2, nt - 1)), dma((2, nt - 1)),
            dma((8,)),
        ],
        compiler_params=pltpu.CompilerParams(collective_id=1, has_side_effects=True),
    )(
        depth_start[0], roughness[0], depth_seed[0], zone_label[0], owner, retention, forcing,
        levee_cell,
    )


def per_device(
    nb, nt, depth_start, roughness, depth_seed, zone_label, owner_slot, retention, forcing,
    levee_cell,
):
    zones = owner_slot.shape[0]
    span = zones // (nb * nt)
    gp = round_up(round_up(span + 1, LANES) // LANES, 8)
    window = (span + LANES - 2) // LANES + 1
    home_rows = round_up(window, 16)
    groups = nb * nt * gp
    digits = 1 if groups <= 256 else 2
    blocks = nb * nt // 2
    rows, cols = depth_start.shape[1:]
    reaches, chains = retention.shape
    padded = round_up(zones, LANES)
    owner = jnp.pad(owner_slot, (0, padded - zones)).reshape(-1, LANES)
    label_groups = round_up(owner.shape[0], LANES)
    deep = rows + 2 * HALO
    vmem = pl.BlockSpec(memory_space=pltpu.VMEM)
    dma = pltpu.SemaphoreType.DMA
    packed = pl.pallas_call(
        functools.partial(main_kernel, nb, nt, span, gp, digits, window),
        out_shape=jax.ShapeDtypeStruct((2 * gp + reaches, LANES), F32),
        in_specs=[pl.BlockSpec(memory_space=pl.ANY)] * 8,
        out_specs=vmem,
        scratch_shapes=[
            pltpu.VMEM((rows, cols), I32),
            pltpu.VMEM(owner.shape, I32),
            pltpu.VMEM((reaches, chains), F32),
            pltpu.VMEM((reaches, chains), F32),
            pltpu.VMEM((reaches, chains), I32),
            pltpu.VMEM((3, deep, cols), F32),
            pltpu.VMEM((LANES, (1 + digits) * label_groups), BF16),
            pltpu.VMEM((label_groups, LANES), F32),
            pltpu.VMEM((label_groups + home_rows, LANES), F32),
            pltpu.VMEM((4, rows, cols), F32),
            pltpu.VMEM((4, rows, cols), F32),
            pltpu.VMEM((8 * ROWS_AT_ONCE, LANES), F32),
            pltpu.VMEM((4 * home_rows, LANES), F32),
            pltpu.VMEM((4, home_rows, LANES), F32),
            pltpu.VMEM((STEPS, rows, cols), F32),
            pltpu.VMEM((STEPS, rows, cols), F32),
            pltpu.VMEM((rows, cols), F32),
            pltpu.VMEM((3 * rows, cols), BF16),
            pltpu.VMEM((reaches, chains), F32),
            pltpu.VMEM((4 * LANES, groups), F32),
            pltpu.VMEM((2, blocks, 2, gp, LANES), F32),
            pltpu.VMEM((blocks, 2, gp, LANES), F32),
            pltpu.VMEM((blocks, 2, gp, LANES), F32),
            pltpu.VMEM((blocks - 1, 2, gp, LANES), F32),
            pltpu.VMEM((nb, 8, chains), F32),
            dma((2, 3)), dma((2, 3)),
            dma((nb - 1,)), dma((nb - 1,)),
            dma, dma,
            dma((blocks - 1,)), dma((blocks - 1,)),
            dma((8,)),
        ],
        compiler_params=pltpu.CompilerParams(collective_id=0, has_side_effects=True),
    )(
        depth_start[0], roughness[0], depth_seed[0], zone_label[0], owner, retention, forcing,
        levee_cell,
    )

    def unpack_with(words, value):
        return pl.pallas_call(
            functools.partial(unpack, words),
            out_shape=(
                jax.ShapeDtypeStruct((words, LANES), F32),
                jax.ShapeDtypeStruct((words, LANES), F32),
                jax.ShapeDtypeStruct((reaches, chains), F32),
            ),
            in_specs=[vmem],
            out_specs=(vmem,) * 3,
        )(value)

    def crowded(value):
        again = full_pass(
            nb, nt, gp, depth_start, roughness, depth_seed, zone_label, owner_slot, retention,
            forcing, levee_cell,
        )
        return unpack_with(gp, again)

    grad, curv, reach = lax.cond(
        packed[gp - 1, LANES - 1] > 0.5, crowded, functools.partial(unpack_with, gp), packed
    )
    return grad.reshape(-1)[:span], curv.reshape(-1)[:span], reach


def solution(mesh):
    in_specs = (
        P("basin", "tile", None),
        P("basin", "tile", None),
        P("basin", "tile", None),
        P("basin", "tile", None),
        P(),
        P("basin", "tile"),
        P("basin", "tile"),
        P("basin", "tile"),
    )
    out_specs = (P(("basin", "tile")), P(("basin", "tile")), P("basin", "tile"))
    return jax.shard_map(
        functools.partial(per_device, mesh.shape["basin"], mesh.shape["tile"]),
        mesh=mesh, in_specs=in_specs, out_specs=out_specs, check_vma=False,
    )
```

```python
import functools

import jax
import jax.numpy as jnp
from jax import lax
from jax.experimental import pallas as pl
from jax.experimental.pallas import tpu as pltpu
from jax.sharding import PartitionSpec as P

STEPS = 4
HALO = 8
LANES = 128
ROWS_AT_ONCE = 8
BATCH = 14

courant = 0.24
rough_ref = 0.025
levee_gain = 0.1

F32 = jnp.float32
BF16 = jnp.bfloat16
I32 = jnp.int32
MESH = pl.DeviceIdType.MESH


def round_up(value, unit):
    return -(-value // unit) * unit


def iota(shape, dim):
    return lax.broadcasted_iota(I32, shape, dim)


def nt_dot(left, right):
    return lax.dot_general(
        left, right, (((1,), (1,)), ((), ())), preferred_element_type=F32
    )


def main_kernel(
    nb, nt, span, gp, digits, window,
    depth_in, rough_in, seed_in, label_hbm, owner_hbm, keep_hbm, force_hbm, cell_hbm,
    packed_out,
    label_in, owner_in, keep_in, force_in, cell_in, ext, table, owner_f, slot_tab, cells, pieces, packed, home_sums, home_parts, diff_e, diff_s, adj_f,
    adj0, levee, hist, sums, pair, part, recv2, maps,
    halo_send, halo_recv, map_send, map_recv, one_send, one_recv, two_send, two_recv, load_sem,
):
    b = lax.axis_index("basin")
    t = lax.axis_index("tile")
    rows, cols = depth_in.shape
    label_groups = table.shape[1] // (1 + digits)
    groups = nb * nt * gp

    blocks = nb * nt // 2
    side = lax.rem(t, 2)
    mine = b * (nt // 2) + t // 2

    def peer(k):
        other = lax.rem(mine + k, blocks)
        return other, (other // (nt // 2), 2 * lax.rem(other, nt // 2) + side)

    barrier = pltpu.get_barrier_semaphore()
    for k in range(1, blocks):
        pl.semaphore_signal(barrier, inc=1, device_id=peer(k)[1], device_id_type=MESH)
    near = sorted({1, nt - 1})
    for k in near:
        pl.semaphore_signal(
            barrier, inc=1, device_id=(b, lax.rem(t + k, nt)), device_id_type=MESH
        )

    fields = (depth_in, rough_in, seed_in)
    pairs = (
        (depth_in, ext.at[0, pl.ds(HALO, rows)]), (rough_in, ext.at[1, pl.ds(HALO, rows)]),
        (seed_in, ext.at[2, pl.ds(HALO, rows)]),
        (owner_hbm, owner_in), (label_hbm, label_in),
        (cell_hbm, cell_in), (keep_hbm, keep_in), (force_hbm, force_in),
    )
    loads = [
        pltpu.make_async_copy(source, target, load_sem.at[index])
        for index, (source, target) in enumerate(pairs)
    ]
    for load in loads:
        load.start()

    def down_copy(f):
        return pltpu.make_async_remote_copy(
            src_ref=fields[f].at[pl.ds(rows - HALO, HALO)],
            dst_ref=ext.at[f, pl.ds(0, HALO)],
            send_sem=halo_send.at[0, f],
            recv_sem=halo_recv.at[0, f],
            device_id=(b, lax.rem(t + 1, nt)),
            device_id_type=MESH,
        )

    def up_copy(f):
        return pltpu.make_async_remote_copy(
            src_ref=fields[f].at[pl.ds(0, HALO)],
            dst_ref=ext.at[f, pl.ds(HALO + rows, HALO)],
            send_sem=halo_send.at[1, f],
            recv_sem=halo_recv.at[1, f],
            device_id=(b, lax.rem(t + nt - 1, nt)),
            device_id_type=MESH,
        )

    def start_halos():
        @pl.when(t < nt - 1)
        def _():
            for f in range(3):
                down_copy(f).start()

        @pl.when(t > 0)
        def _():
            for f in range(3):
                up_copy(f).start()

    def right(v):
        return pltpu.roll(v, cols - 1, 1)

    def from_left(v):
        return pltpu.roll(v, 1, 1)

    def sweep(depth, rough, adjoint, mask_rows):
        deep = depth.shape[0]
        face_e = iota((deep, cols), 1) < cols - 1

        def below(v):
            return pltpu.roll(v, deep - 1, 0)

        def from_above(v):
            return pltpu.roll(v, 1, 0)

        conduct = rough_ref / rough
        inner = face_s = None
        if mask_rows is not None:
            inner, face_s = mask_rows
            conduct = jnp.where(inner, conduct, 0.0)
        weight_e = jnp.where(face_e, (0.5 * courant) * (conduct + right(conduct)), 0.0)
        weight_s = (0.5 * courant) * (conduct + below(conduct))
        if face_s is not None:
            weight_s = jnp.where(face_s, weight_s, 0.0)

        def advance(v, de, ds):
            flow_e = weight_e * de
            flow_s = weight_s * ds
            return v + ((flow_e - from_left(flow_e)) + (flow_s - from_above(flow_s)))

        for s in range(STEPS):
            de = right(depth) - depth
            ds = below(depth) - depth
            diff_e[s, pl.ds(0, deep)] = de
            diff_s[s, pl.ds(0, deep)] = ds
            if s < STEPS - 1:
                depth = advance(depth, de, ds)
        prod_e = jnp.zeros((deep, cols), F32)
        prod_s = jnp.zeros((deep, cols), F32)
        for s in reversed(range(STEPS)):
            de = right(adjoint) - adjoint
            ds = below(adjoint) - adjoint
            prod_e = prod_e + diff_e[s, pl.ds(0, deep)] * de
            prod_s = prod_s + diff_s[s, pl.ds(0, deep)] * ds
            adjoint = advance(adjoint, de, ds)
        prod_e = jnp.where(face_e, prod_e, 0.0)
        if face_s is not None:
            prod_s = jnp.where(face_s, prod_s, 0.0)
        product = (prod_e + from_left(prod_e)) + (prod_s + from_above(prod_s))
        gradient = (0.5 * courant) * conduct * product
        square = gradient * gradient
        parts = []
        for value in (gradient, square):
            high = value.astype(BF16).astype(F32)
            parts += [high, value - high]
        return parts, adjoint

    def interior():
        parts, adjoint = sweep(*(ext[f, pl.ds(HALO, rows)] for f in range(3)), None)
        for index, value in enumerate(parts):
            pieces[index] = value
        adj_f[...] = adjoint

    def edges():
        @pl.when(t < nt - 1)
        def _():
            for f in range(3):
                down_copy(f).wait_send()
                up_copy(f).wait_recv()

        @pl.when(t > 0)
        def _():
            for f in range(3):
                up_copy(f).wait_send()
                down_copy(f).wait_recv()

        @pl.when(t == 0)
        def _():
            for f in range(3):
                ext[f, pl.ds(0, HALO)] = jnp.ones((HALO, cols), F32)

        @pl.when(t == nt - 1)
        def _():
            for f in range(3):
                ext[f, pl.ds(HALO + rows, HALO)] = jnp.ones((HALO, cols), F32)

        strip = 2 * HALO
        local = iota((2 * strip, cols), 0)
        row_id = jnp.where(local < strip, local, local + (rows - strip))
        first = jnp.where(t == 0, HALO, 0)
        last = jnp.where(t == nt - 1, HALO + rows - 1, rows + 2 * HALO - 1)
        masks = (
            (row_id >= first) & (row_id <= last), (row_id >= first) & (row_id < last)
        )
        parts, adjoint = sweep(
            *(
                jnp.concatenate([ext[f, pl.ds(0, strip)], ext[f, pl.ds(rows, strip)]], axis=0)
                for f in range(3)
            ),
            masks,
        )
        low = strip + HALO - STEPS
        for index, value in enumerate(parts):
            pieces[index, pl.ds(0, STEPS)] = value[HALO : HALO + STEPS]
            pieces[index, pl.ds(rows - STEPS, STEPS)] = value[low : low + STEPS]
        adj_f[pl.ds(0, STEPS)] = adjoint[HALO : HALO + STEPS]
        adj_f[pl.ds(rows - STEPS, STEPS)] = adjoint[low : low + STEPS]
    for load in loads[:3]:
        load.wait()
    interior()
    loads[3].wait()
    owner = owner_in[...].astype(F32)
    device = jnp.floor((owner + 0.5) * (1.0 / span))
    inside = owner - device * span
    block = jnp.floor(inside * (1.0 / LANES))
    group = device * gp + block
    lane = inside - block * LANES
    owner_f[...] = jnp.zeros(owner_f.shape, F32)
    slot_tab[...] = jnp.zeros(slot_tab.shape, F32)
    held = owner.shape[0]
    slot_tab[pl.ds(0, held)] = group * LANES + lane
    parts = [lane]
    for digit in range(digits):
        upper = jnp.floor(group * (1.0 / 256.0))
        parts.append((group - upper * 256.0) * float(LANES * 256**digit))
        group = upper
    for index, value in enumerate(parts):
        owner_f[pl.ds(0, held)] = value
        table[:, pl.ds(index * label_groups, label_groups)] = owner_f[...].T.astype(BF16)
    count = iota((256, LANES), 0).astype(F32).astype(BF16)

    def spread_rows(row, size):
        tall = jnp.broadcast_to(row, (16, LANES)).astype(BF16)
        return tall if size == 16 else jnp.concatenate([tall] * (size // 16), axis=0)

    def row_of(ref, row):
        return ref[pl.ds(row, 1), :]

    def hot_rows(size, index):
        if size > 256:
            return jnp.where(iota((size, LANES), 0) == index.astype(I32), 1.0, 0.0).astype(BF16)
        return jnp.where(count[:size] == spread_rows(index, size), BF16(1), BF16(0))

    def side_by_side(pieces_of_row):
        return jnp.concatenate(pieces_of_row, axis=1)

    dev = b * nt + t
    first_group = (dev * span) // LANES
    home_rows = round_up(window, 16)
    per_group = 2 if cols % (2 * LANES) == 0 else 1
    places = LANES * LANES * per_group // cols

    def prepare():
        labels = label_in[...]
        group_of = lax.shift_right_logical(labels, 7)
        place = group_of - first_group
        stray = (place < 0) | (place >= window)
        wide = per_group * LANES
        before = jnp.where(iota((wide, wide), 0) <= iota((wide, wide), 1), 1.0, 0.0).astype(BF16)
        odd = jnp.where(stray, 1.0, 0.0).astype(BF16)
        rank = side_by_side(
            [
                jnp.dot(odd[:, k : k + wide], before, preferred_element_type=F32)
                for k in range(0, cols, wide)
            ]
        )
        cells[0] = group_of.astype(F32)
        cells[1] = jnp.bitwise_and(labels, LANES - 1).astype(F32)
        cells[2] = jnp.where(stray, -1.0, place.astype(F32))
        cells[3] = jnp.where(stray, rank - 1.0, -1.0)
        most = jnp.max(jnp.max(rank, axis=0, keepdims=True), axis=1, keepdims=True)
        over = jnp.where(most > places, 1.0, 0.0)
        hist[...] = jnp.zeros(hist.shape, F32)
        spare = (lax.rem(iota((groups, LANES), 0), gp) == gp - 1) & (
            iota((groups, LANES), 1) == LANES - 1
        )
        hist[:, pl.ds(0, LANES)] = jnp.where(spare, over, 0.0)
        home_sums[...] = jnp.zeros(home_sums.shape, F32)

    def compact(rows_of_chunk):
        line = count[:16]
        home_left, home_right = [], []
        for q, row in enumerate(rows_of_chunk):
            left, right_side = [], []
            labels = [cells[i, pl.ds(row, 1), :] for i in range(4)]
            amounts = [pieces[i, pl.ds(row, 1), :] for i in range(4)]
            for c in range(0, cols, LANES):
                upper, lower, place, position = (v[:, c : c + LANES] for v in labels)
                values = [spread_rows(v[:, c : c + LANES], 16) for v in amounts]
                right_side.append(hot_rows(places, position))
                home_right.append(hot_rows(LANES, lower))
                carried = BF16(0)
                for i, value in enumerate([spread_rows(upper, 16), spread_rows(lower, 16)] + values):
                    carried = jnp.where(line == BF16(i), value, carried)
                weighted = []
                for first_row in range(0, home_rows, 16):
                    mask = count[first_row : first_row + 16] == spread_rows(place, 16)
                    weighted.append([jnp.where(mask, value, BF16(0)) for value in values])
                left.append(carried)
                home_left.append(
                    jnp.concatenate([part_of[i] for i in range(4) for part_of in weighted], axis=0)
                )
            found = side_by_side(
                [
                    nt_dot(
                        side_by_side(left[k : k + per_group]), side_by_side(right_side[k : k + per_group])
                    )
                    for k in range(0, len(left), per_group)
                ]
            )
            packed[pl.ds(8 * q, 8)] = found[:8]
        home_sums[...] += nt_dot(side_by_side(home_right), side_by_side(home_left))

    def add_to_slots(slots, values_of):
        hot_groups = []
        weighted = []
        for slot, values in zip(slots, values_of):
            index = slot.astype(I32)
            hot_groups.append(hot_rows(groups, lax.shift_right_logical(index, 7).astype(F32)))
            lane_row = jnp.bitwise_and(index, LANES - 1).astype(F32)
            mask = count[:LANES] == spread_rows(lane_row, LANES)
            weighted.append(
                jnp.concatenate(
                    [jnp.where(mask, spread_rows(v, LANES), BF16(0)) for v in values], axis=0
                )
            )
        hist[...] += nt_dot(side_by_side(hot_groups), side_by_side(weighted))

    def stray_sums(size):
        hot = side_by_side([hot_rows(label_groups, row_of(packed, 8 * q)) for q in range(size)])
        found = jnp.dot(
            table[...], jnp.concatenate([hot] * (1 + digits), axis=0), preferred_element_type=F32
        )
        slots = []
        for q in range(size):
            mask = iota((LANES, LANES), 0) == row_of(packed, 8 * q + 1).astype(I32)
            slots.append(
                jnp.sum(
                    jnp.where(mask, found[:, q * LANES : (q + 1) * LANES], 0.0),
                    axis=0, keepdims=True,
                )
            )
        return slots, [[row_of(packed, 8 * q + 2 + i) for i in range(4)] for q in range(size)]

    def home_totals():
        homes_t = home_sums[...].T
        for which in range(2):
            low = 2 * which * home_rows
            value = (homes_t[low : low + home_rows] + homes_t[low + home_rows : low + 2 * home_rows])
            high = value.astype(BF16).astype(F32)
            home_parts[2 * which] = high
            home_parts[2 * which + 1] = value - high
        return (
            [row_of(slot_tab, first_group + i) for i in range(window)],
            [[home_parts[k, pl.ds(i, 1), :] for k in range(4)] for i in range(window)],
        )

    loads[4].wait()
    chunks = rows // ROWS_AT_ONCE
    half = ROWS_AT_ONCE // 2
    batch = packed.shape[0] // 8

    def inner_chunk(chunk, unused):
        compact([half + chunk * batch + q for q in range(batch)])
        add_to_slots(*stray_sums(batch))
        return unused

    prepare()
    steps = (rows - ROWS_AT_ONCE) // batch
    early = steps // 2
    lax.fori_loop(0, early, inner_chunk, 0)
    pl.semaphore_wait(barrier, blocks - 1 + len(near))
    start_halos()
    lax.fori_loop(early, steps, inner_chunk, 0)
    for load in loads[5:]:
        load.wait()

    def pair_copy():
        return pltpu.make_async_remote_copy(
            src_ref=sums.at[1 - side],
            dst_ref=pair,
            send_sem=one_send,
            recv_sem=one_recv,
            device_id=(b, t + 1 - 2 * side),
            device_id_type=MESH,
        )

    def two_copy(k):
        other, device = peer(k)
        return pltpu.make_async_remote_copy(
            src_ref=part.at[other],
            dst_ref=recv2.at[k - 1],
            send_sem=two_send.at[k - 1],
            recv_sem=two_recv.at[k - 1],
            device_id=device,
            device_id_type=MESH,
        )

    edges()
    compact([q if q < half else rows - ROWS_AT_ONCE + q for q in range(ROWS_AT_ONCE)])
    strays, homes = stray_sums(ROWS_AT_ONCE), home_totals()
    add_to_slots(strays[0] + homes[0], strays[1] + homes[1])
    for which in range(2):
        low = 2 * which * LANES
        total = hist[:, pl.ds(low, LANES)] + hist[:, pl.ds(low + LANES, LANES)]
        total = total.reshape(blocks, 2, gp, LANES)
        for p in range(2):
            sums[p, :, which] = total[:, p]
    pair_copy().start()
    rest = adj_f[...]
    for piece in range(3):
        high = rest.astype(BF16)
        adj0[pl.ds(piece * rows, rows)] = high
        rest = rest - high.astype(F32)
    pair_copy().wait()
    part[...] = sums[side] + pair[...]
    for k in range(1, blocks):
        two_copy(k).start()
    reaches, chains = cell_in.shape
    shift = cols.bit_length() - 1

    def levees(chunk, unused):
        base = chunk * 4
        cells = jnp.concatenate([row_of(cell_in, base + q) for q in range(4)], axis=1)
        wide = 4 * chains
        column = jnp.bitwise_and(cells, cols - 1)
        line = lax.shift_right_logical(cells, shift)
        hot = jnp.where(iota((cols, wide), 0) == column, 1.0, 0.0).astype(BF16)
        picked = jnp.dot(adj0[...], hot, preferred_element_type=F32)
        picked = (picked[:rows] + picked[rows : 2 * rows]) + picked[2 * rows :]
        value = jnp.sum(
            jnp.where(iota((rows, wide), 0) == line, picked, 0.0), axis=0, keepdims=True
        )
        for q in range(4):
            levee[pl.ds(base + q, 1), :] = value[:, q * chains : (q + 1) * chains]
        return unused

    lax.fori_loop(0, reaches // 4, levees, 0)

    rate = keep_in[...]
    push = force_in[...] + levee_gain * levee[...]
    reach_id = iota((reaches, chains), 0)
    step = 1
    while step < reaches:
        has = reach_id < reaches - step
        next_rate = jnp.where(has, pltpu.roll(rate, reaches - step, 0), 1.0)
        next_push = jnp.where(has, pltpu.roll(push, reaches - step, 0), 0.0)
        push = push + rate * next_push
        rate = rate * next_rate
        step *= 2
    maps[0, pl.ds(0, 1)] = rate[0:1]
    maps[0, pl.ds(1, 1)] = push[0:1]
    maps[0, pl.ds(2, 6)] = jnp.zeros((6, chains), F32)

    def map_copy(k):
        return pltpu.make_async_remote_copy(
            src_ref=maps.at[0],
            dst_ref=maps.at[k],
            send_sem=map_send.at[k - 1],
            recv_sem=map_recv.at[k - 1],
            device_id=(lax.rem(b + k, nb), t),
            device_id_type=MESH,
        )

    for k in range(1, nb):
        map_copy(k).start()

    for k in range(1, nb):
        map_copy(k).wait()
    incoming = jnp.zeros((1, chains), F32)
    for other in reversed(range(nb)):
        slot = lax.rem(b - other + nb, nb)
        stretch = maps[slot]
        incoming = jnp.where(
            other > b, stretch[0:1] * incoming + stretch[1:2], incoming
        )
    packed_out[pl.ds(2 * gp, reaches)] = rate * incoming + push
    for k in range(1, blocks):
        two_copy(k).wait()
    total = part[mine]
    for k in range(1, blocks):
        total = total + recv2[k - 1]
    for which in range(2):
        packed_out[pl.ds(which * gp, gp)] = total[which]


def full_kernel(
    nb, nt, span, gp, digits,
    depth_in, rough_in, seed_in, label_hbm, owner_hbm, keep_hbm, force_hbm, cell_hbm,
    packed_out,
    label_in, owner_in, keep_in, force_in, cell_in, ext, table, owner_f, slot_s, pieces, diff_e, diff_s, adj0, levee,
    hist, sums, recv1, part, recv2, maps,
    halo_send, halo_recv, map_send, map_recv, one_send, one_recv, two_send, two_recv, load_sem,
):
    b = lax.axis_index("basin")
    t = lax.axis_index("tile")
    rows, cols = depth_in.shape
    label_groups = table.shape[1] // (1 + digits)
    groups = nb * nt * gp

    barrier = pltpu.get_barrier_semaphore()
    for k in range(1, nb):
        pl.semaphore_signal(
            barrier, inc=1, device_id=(lax.rem(b + k, nb), t), device_id_type=MESH
        )
    for k in range(1, nt):
        pl.semaphore_signal(
            barrier, inc=1, device_id=(b, lax.rem(t + k, nt)), device_id_type=MESH
        )

    fields = (depth_in, rough_in, seed_in)
    pairs = (
        (owner_hbm, owner_in), (label_hbm, label_in),
        (depth_in, ext.at[0, pl.ds(HALO, rows)]), (rough_in, ext.at[1, pl.ds(HALO, rows)]),
        (seed_in, ext.at[2, pl.ds(HALO, rows)]),
        (cell_hbm, cell_in), (keep_hbm, keep_in), (force_hbm, force_in),
    )
    loads = [
        pltpu.make_async_copy(source, target, load_sem.at[index])
        for index, (source, target) in enumerate(pairs)
    ]
    for load in loads:
        load.start()
    pl.semaphore_wait(barrier, nb - 1 + nt - 1)

    def down_copy(f):
        return pltpu.make_async_remote_copy(
            src_ref=fields[f].at[pl.ds(rows - HALO, HALO)],
            dst_ref=ext.at[f, pl.ds(0, HALO)],
            send_sem=halo_send.at[0, f],
            recv_sem=halo_recv.at[0, f],
            device_id=(b, lax.rem(t + 1, nt)),
            device_id_type=MESH,
        )

    def up_copy(f):
        return pltpu.make_async_remote_copy(
            src_ref=fields[f].at[pl.ds(0, HALO)],
            dst_ref=ext.at[f, pl.ds(HALO + rows, HALO)],
            send_sem=halo_send.at[1, f],
            recv_sem=halo_recv.at[1, f],
            device_id=(b, lax.rem(t + nt - 1, nt)),
            device_id_type=MESH,
        )

    @pl.when(t < nt - 1)
    def _():
        for f in range(3):
            down_copy(f).start()

    @pl.when(t > 0)
    def _():
        for f in range(3):
            up_copy(f).start()

    loads[0].wait()
    owner = owner_in[...].astype(F32)
    device = jnp.floor((owner + 0.5) * (1.0 / span))
    inside = owner - device * span
    block = jnp.floor(inside * (1.0 / LANES))
    group = device * gp + block
    lane = inside - block * LANES
    owner_f[...] = jnp.zeros(owner_f.shape, F32)
    held = owner.shape[0]
    parts = [lane]
    for digit in range(digits):
        upper = jnp.floor(group * (1.0 / 256.0))
        parts.append((group - upper * 256.0) * float(LANES * 256**digit))
        group = upper
    for index, value in enumerate(parts):
        owner_f[pl.ds(0, held)] = value
        table[:, pl.ds(index * label_groups, label_groups)] = owner_f[...].T.astype(BF16)
    count = iota((256, LANES), 0).astype(F32).astype(BF16)

    def spread_rows(row, size):
        tall = jnp.broadcast_to(row, (16, LANES)).astype(BF16)
        return jnp.concatenate([tall] * (size // 16), axis=0)

    def row_of(ref, row):
        return ref[pl.ds(row, 1), :]

    def hot_rows(size, index):
        if size > 256:
            return jnp.where(iota((size, cols), 0) == index, 1.0, 0.0).astype(BF16)
        narrow = index.astype(F32)
        return jnp.concatenate(
            [
                jnp.where(
                    count[:size] == spread_rows(narrow[:, c : c + LANES], size), BF16(1), BF16(0)
                )
                for c in range(0, cols, LANES)
            ],
            axis=1,
        )

    def look_up(chunk, unused):
        for q in range(ROWS_AT_ONCE):
            row = chunk * ROWS_AT_ONCE + q
            labels = row_of(label_in, row)
            hot = hot_rows(label_groups, lax.shift_right_logical(labels, 7))
            found = jnp.dot(
                table[...],
                jnp.concatenate([hot] * (1 + digits), axis=0),
                preferred_element_type=F32,
            )
            mask = iota((LANES, cols), 0) == jnp.bitwise_and(labels, LANES - 1)
            slot_s[pl.ds(row, 1), :] = jnp.sum(
                jnp.where(mask, found, 0.0), axis=0, keepdims=True
            )
        return unused

    loads[1].wait()
    lax.fori_loop(0, rows // ROWS_AT_ONCE, look_up, 0)
    for load in loads[2:]:
        load.wait()

    @pl.when(t < nt - 1)
    def _():
        for f in range(3):
            down_copy(f).wait_send()
            up_copy(f).wait_recv()

    @pl.when(t > 0)
    def _():
        for f in range(3):
            up_copy(f).wait_send()
            down_copy(f).wait_recv()

    @pl.when(t == 0)
    def _():
        for f in range(3):
            ext[f, pl.ds(0, HALO)] = jnp.ones((HALO, cols), F32)

    @pl.when(t == nt - 1)
    def _():
        for f in range(3):
            ext[f, pl.ds(HALO + rows, HALO)] = jnp.ones((HALO, cols), F32)

    deep = rows + 2 * HALO
    row_id = iota((deep, cols), 0)
    col_id = iota((deep, cols), 1)
    first = jnp.where(t == 0, HALO, 0)
    last = jnp.where(t == nt - 1, HALO + rows - 1, deep - 1)
    inner = (row_id >= first) & (row_id <= last)
    face_s = (row_id >= first) & (row_id < last)
    face_e = col_id < cols - 1

    def below(v):
        return pltpu.roll(v, deep - 1, 0)

    def right(v):
        return pltpu.roll(v, cols - 1, 1)

    def from_above(v):
        return pltpu.roll(v, 1, 0)

    def from_left(v):
        return pltpu.roll(v, 1, 1)

    conduct = jnp.where(inner, rough_ref / ext[1], 0.0)
    weight_e = jnp.where(face_e, (0.5 * courant) * (conduct + right(conduct)), 0.0)
    weight_s = jnp.where(face_s, (0.5 * courant) * (conduct + below(conduct)), 0.0)

    def advance(v, de, ds):
        flow_e = weight_e * de
        flow_s = weight_s * ds
        return v + ((flow_e - from_left(flow_e)) + (flow_s - from_above(flow_s)))

    depth = ext[0]
    for s in range(STEPS):
        de = right(depth) - depth
        ds = below(depth) - depth
        diff_e[s] = de
        diff_s[s] = ds
        if s < STEPS - 1:
            depth = advance(depth, de, ds)
    adjoint = ext[2]
    prod_e = jnp.zeros((deep, cols), F32)
    prod_s = jnp.zeros((deep, cols), F32)
    for s in reversed(range(STEPS)):
        de = right(adjoint) - adjoint
        ds = below(adjoint) - adjoint
        prod_e = prod_e + diff_e[s] * de
        prod_s = prod_s + diff_s[s] * ds
        adjoint = advance(adjoint, de, ds)
    prod_e = jnp.where(face_e, prod_e, 0.0)
    prod_s = jnp.where(face_s, prod_s, 0.0)
    product = (prod_e + from_left(prod_e)) + (prod_s + from_above(prod_s))
    gradient = ((0.5 * courant) * conduct * product)[HALO : HALO + rows]
    square = gradient * gradient
    for index, value in enumerate((gradient, square)):
        high = value.astype(BF16).astype(F32)
        pieces[2 * index] = high
        pieces[2 * index + 1] = value - high

    def gather_rows(which, chunk, unused):
        hot_groups = []
        weighted = []
        for q in range(ROWS_AT_ONCE):
            row = chunk * ROWS_AT_ONCE + q
            slot = row_of(slot_s, row).astype(I32)
            hot_groups.append(hot_rows(groups, lax.shift_right_logical(slot, 7)))
            lane_row = jnp.bitwise_and(slot, LANES - 1).astype(F32)
            values = [pieces[i, pl.ds(row, 1), :] for i in range(4)]
            masked = []
            for c in range(0, cols, LANES):
                mask = count[:LANES] == spread_rows(lane_row[:, c : c + LANES], LANES)
                masked.append(
                    jnp.concatenate(
                        [
                            jnp.where(mask, spread_rows(v[:, c : c + LANES], LANES), BF16(0))
                            for v in values
                        ],
                        axis=0,
                    )
                )
            weighted.append(jnp.concatenate(masked, axis=1))
        hist[...] += nt_dot(
            jnp.concatenate(weighted, axis=1), jnp.concatenate(hot_groups, axis=1)
        )
        return unused

    chunks = rows // ROWS_AT_ONCE

    def one_copy(which, k):
        other = lax.rem(b + k, nb)
        return pltpu.make_async_remote_copy(
            src_ref=sums.at[which, pl.ds(pl.multiple_of(other * (nt * gp), 8), nt * gp)],
            dst_ref=recv1.at[k - 1, which],
            send_sem=one_send.at[which, k - 1],
            recv_sem=one_recv.at[which, k - 1],
            device_id=(other, t),
            device_id_type=MESH,
        )

    def two_copy(which, k):
        other = lax.rem(t + k, nt)
        return pltpu.make_async_remote_copy(
            src_ref=part.at[which, pl.ds(pl.multiple_of(other * gp, 8), gp)],
            dst_ref=recv2.at[k - 1, which],
            send_sem=two_send.at[which, k - 1],
            recv_sem=two_recv.at[which, k - 1],
            device_id=(b, other),
            device_id_type=MESH,
        )

    def collect(which, start, stop):
        lax.fori_loop(start, stop, functools.partial(gather_rows, which), 0)

    def first_phase(which):
        sums[which] = (hist[pl.ds(2 * which * LANES, LANES)] + hist[pl.ds((2 * which + 1) * LANES, LANES)]).T
        for k in range(1, nb):
            one_copy(which, k).start()

    def second_phase(which):
        for k in range(1, nb):
            one_copy(which, k).wait()
        total = sums[which, pl.ds(pl.multiple_of(b * (nt * gp), 8), nt * gp)]
        for k in range(1, nb):
            total = total + recv1[k - 1, which]
        part[which] = total
        for k in range(1, nt):
            two_copy(which, k).start()

    def finish(which):
        for k in range(1, nt):
            two_copy(which, k).wait()
        total = part[which, pl.ds(pl.multiple_of(t * gp, 8), gp)]
        for k in range(1, nt):
            total = total + recv2[k - 1, which]
        packed_out[pl.ds(which * gp, gp)] = total

    hist[...] = jnp.zeros(hist.shape, F32)
    collect(0, 0, chunks)
    first_phase(0)
    first_phase(1)
    rest = adjoint[HALO : HALO + rows]
    for piece in range(3):
        high = rest.astype(BF16)
        adj0[pl.ds(piece * rows, rows)] = high
        rest = rest - high.astype(F32)
    reaches, chains = cell_in.shape
    shift = cols.bit_length() - 1

    def levees(chunk, unused):
        base = chunk * 4
        cells = jnp.concatenate([row_of(cell_in, base + q) for q in range(4)], axis=1)
        wide = 4 * chains
        column = jnp.bitwise_and(cells, cols - 1)
        line = lax.shift_right_logical(cells, shift)
        hot = jnp.where(iota((cols, wide), 0) == column, 1.0, 0.0).astype(BF16)
        picked = jnp.dot(adj0[...], hot, preferred_element_type=F32)
        picked = (picked[:rows] + picked[rows : 2 * rows]) + picked[2 * rows :]
        value = jnp.sum(
            jnp.where(iota((rows, wide), 0) == line, picked, 0.0), axis=0, keepdims=True
        )
        for q in range(4):
            levee[pl.ds(base + q, 1), :] = value[:, q * chains : (q + 1) * chains]
        return unused

    lax.fori_loop(0, reaches // 4, levees, 0)

    rate = keep_in[...]
    push = force_in[...] + levee_gain * levee[...]
    reach_id = iota((reaches, chains), 0)
    step = 1
    while step < reaches:
        has = reach_id < reaches - step
        next_rate = jnp.where(has, pltpu.roll(rate, reaches - step, 0), 1.0)
        next_push = jnp.where(has, pltpu.roll(push, reaches - step, 0), 0.0)
        push = push + rate * next_push
        rate = rate * next_rate
        step *= 2
    maps[0, pl.ds(0, 1)] = rate[0:1]
    maps[0, pl.ds(1, 1)] = push[0:1]
    maps[0, pl.ds(2, 6)] = jnp.zeros((6, chains), F32)

    def map_copy(k):
        return pltpu.make_async_remote_copy(
            src_ref=maps.at[0],
            dst_ref=maps.at[k],
            send_sem=map_send.at[k - 1],
            recv_sem=map_recv.at[k - 1],
            device_id=(lax.rem(b + k, nb), t),
            device_id_type=MESH,
        )

    for k in range(1, nb):
        map_copy(k).start()

    second_phase(0)
    second_phase(1)
    for k in range(1, nb):
        map_copy(k).wait()
    incoming = jnp.zeros((1, chains), F32)
    for other in reversed(range(nb)):
        slot = lax.rem(b - other + nb, nb)
        stretch = maps[slot]
        incoming = jnp.where(
            other > b, stretch[0:1] * incoming + stretch[1:2], incoming
        )
    packed_out[pl.ds(2 * gp, reaches)] = rate * incoming + push
    finish(0)
    finish(1)


def unpack(gp, packed_in, grad_out, curv_out, reach_out):
    grad_out[...] = packed_in[pl.ds(0, gp)]
    curv_out[...] = packed_in[pl.ds(gp, gp)]
    reach_out[...] = packed_in[pl.ds(2 * gp, reach_out.shape[0])]


def full_pass(
    nb, nt, gp, depth_start, roughness, depth_seed, zone_label, owner_slot, retention, forcing,
    levee_cell,
):
    zones = owner_slot.shape[0]
    span = zones // (nb * nt)
    groups = nb * nt * gp
    digits = 1 if groups <= 256 else 2
    rows, cols = depth_start.shape[1:]
    reaches, chains = retention.shape
    padded = round_up(zones, LANES)
    owner = jnp.pad(owner_slot, (0, padded - zones)).reshape(-1, LANES)
    label_groups = round_up(owner.shape[0], LANES)
    deep = rows + 2 * HALO
    vmem = pl.BlockSpec(memory_space=pltpu.VMEM)
    dma = pltpu.SemaphoreType.DMA
    return pl.pallas_call(
        functools.partial(full_kernel, nb, nt, span, gp, digits),
        out_shape=jax.ShapeDtypeStruct((2 * gp + reaches, LANES), F32),
        in_specs=[pl.BlockSpec(memory_space=pl.ANY)] * 8,
        out_specs=vmem,
        scratch_shapes=[
            pltpu.VMEM((rows, cols), I32),
            pltpu.VMEM(owner.shape, I32),
            pltpu.VMEM((reaches, chains), F32),
            pltpu.VMEM((reaches, chains), F32),
            pltpu.VMEM((reaches, chains), I32),
            pltpu.VMEM((3, deep, cols), F32),
            pltpu.VMEM((LANES, (1 + digits) * label_groups), BF16),
            pltpu.VMEM((label_groups, LANES), F32),
            pltpu.VMEM((rows, cols), F32),
            pltpu.VMEM((4, rows, cols), F32),
            pltpu.VMEM((STEPS, deep, cols), F32),
            pltpu.VMEM((STEPS, deep, cols), F32),
            pltpu.VMEM((3 * rows, cols), BF16),
            pltpu.VMEM((reaches, chains), F32),
            pltpu.VMEM((4 * LANES, groups), F32),
            pltpu.VMEM((2, groups, LANES), F32),
            pltpu.VMEM((nb - 1, 2, nt * gp, LANES), F32),
            pltpu.VMEM((2, nt * gp, LANES), F32),
            pltpu.VMEM((nt - 1, 2, gp, LANES), F32),
            pltpu.VMEM((nb, 8, chains), F32),
            dma((2, 3)), dma((2, 3)),
            dma((nb - 1,)), dma((nb - 1,)),
            dma((2, nb - 1)), dma((2, nb - 1)),
            dma((2, nt - 1)), dma((2, nt - 1)),
            dma((8,)),
        ],
        compiler_params=pltpu.CompilerParams(collective_id=1, has_side_effects=True),
    )(
        depth_start[0], roughness[0], depth_seed[0], zone_label[0], owner, retention, forcing,
        levee_cell,
    )


def per_device(
    nb, nt, depth_start, roughness, depth_seed, zone_label, owner_slot, retention, forcing,
    levee_cell,
):
    zones = owner_slot.shape[0]
    span = zones // (nb * nt)
    gp = round_up(round_up(span + 1, LANES) // LANES, 8)
    window = (span + LANES - 2) // LANES + 1
    home_rows = round_up(window, 16)
    batch = max(n for n in range(1, BATCH + 1) if (depth_start.shape[1] - ROWS_AT_ONCE) % n == 0)
    groups = nb * nt * gp
    digits = 1 if groups <= 256 else 2
    blocks = nb * nt // 2
    rows, cols = depth_start.shape[1:]
    reaches, chains = retention.shape
    padded = round_up(zones, LANES)
    owner = jnp.pad(owner_slot, (0, padded - zones)).reshape(-1, LANES)
    label_groups = round_up(owner.shape[0], LANES)
    deep = rows + 2 * HALO
    vmem = pl.BlockSpec(memory_space=pltpu.VMEM)
    dma = pltpu.SemaphoreType.DMA
    packed = pl.pallas_call(
        functools.partial(main_kernel, nb, nt, span, gp, digits, window),
        out_shape=jax.ShapeDtypeStruct((2 * gp + reaches, LANES), F32),
        in_specs=[pl.BlockSpec(memory_space=pl.ANY)] * 8,
        out_specs=vmem,
        scratch_shapes=[
            pltpu.VMEM((rows, cols), I32),
            pltpu.VMEM(owner.shape, I32),
            pltpu.VMEM((reaches, chains), F32),
            pltpu.VMEM((reaches, chains), F32),
            pltpu.VMEM((reaches, chains), I32),
            pltpu.VMEM((3, deep, cols), F32),
            pltpu.VMEM((LANES, (1 + digits) * label_groups), BF16),
            pltpu.VMEM((label_groups, LANES), F32),
            pltpu.VMEM((label_groups + home_rows, LANES), F32),
            pltpu.VMEM((4, rows, cols), F32),
            pltpu.VMEM((4, rows, cols), F32),
            pltpu.VMEM((8 * batch, LANES), F32),
            pltpu.VMEM((LANES, 4 * home_rows), F32),
            pltpu.VMEM((4, home_rows, LANES), F32),
            pltpu.VMEM((STEPS, rows, cols), F32),
            pltpu.VMEM((STEPS, rows, cols), F32),
            pltpu.VMEM((rows, cols), F32),
            pltpu.VMEM((3 * rows, cols), BF16),
            pltpu.VMEM((reaches, chains), F32),
            pltpu.VMEM((groups, 4 * LANES), F32),
            pltpu.VMEM((2, blocks, 2, gp, LANES), F32),
            pltpu.VMEM((blocks, 2, gp, LANES), F32),
            pltpu.VMEM((blocks, 2, gp, LANES), F32),
            pltpu.VMEM((blocks - 1, 2, gp, LANES), F32),
            pltpu.VMEM((nb, 8, chains), F32),
            dma((2, 3)), dma((2, 3)),
            dma((nb - 1,)), dma((nb - 1,)),
            dma, dma,
            dma((blocks - 1,)), dma((blocks - 1,)),
            dma((8,)),
        ],
        compiler_params=pltpu.CompilerParams(collective_id=0, has_side_effects=True),
    )(
        depth_start[0], roughness[0], depth_seed[0], zone_label[0], owner, retention, forcing,
        levee_cell,
    )

    def unpack_with(words, value):
        return pl.pallas_call(
            functools.partial(unpack, words),
            out_shape=(
                jax.ShapeDtypeStruct((words, LANES), F32),
                jax.ShapeDtypeStruct((words, LANES), F32),
                jax.ShapeDtypeStruct((reaches, chains), F32),
            ),
            in_specs=[vmem],
            out_specs=(vmem,) * 3,
        )(value)

    def crowded(value):
        again = full_pass(
            nb, nt, gp, depth_start, roughness, depth_seed, zone_label, owner_slot, retention,
            forcing, levee_cell,
        )
        return unpack_with(gp, again)

    grad, curv, reach = lax.cond(
        packed[gp - 1, LANES - 1] > 0.5, crowded, functools.partial(unpack_with, gp), packed
    )
    return grad.reshape(-1)[:span], curv.reshape(-1)[:span], reach


def solution(mesh):
    in_specs = (
        P("basin", "tile", None),
        P("basin", "tile", None),
        P("basin", "tile", None),
        P("basin", "tile", None),
        P(),
        P("basin", "tile"),
        P("basin", "tile"),
        P("basin", "tile"),
    )
    out_specs = (P(("basin", "tile")), P(("basin", "tile")), P("basin", "tile"))
    return jax.shard_map(
        functools.partial(per_device, mesh.shape["basin"], mesh.shape["tile"]),
        mesh=mesh, in_specs=in_specs, out_specs=out_specs, check_vma=False,
    )
```

```python
import functools

import jax
import jax.numpy as jnp
from jax import lax
from jax.experimental import pallas as pl
from jax.experimental.pallas import tpu as pltpu
from jax.sharding import PartitionSpec as P

STEPS = 4
HALO = 8
LANES = 128
ROWS_AT_ONCE = 8
BATCH = 16
EARLY = 2

courant = 0.24
rough_ref = 0.025
levee_gain = 0.1

F32 = jnp.float32
BF16 = jnp.bfloat16
I32 = jnp.int32
MESH = pl.DeviceIdType.MESH


def round_up(value, unit):
    return -(-value // unit) * unit


def iota(shape, dim):
    return lax.broadcasted_iota(I32, shape, dim)


def nt_dot(left, right):
    return lax.dot_general(
        left, right, (((1,), (1,)), ((), ())), preferred_element_type=F32
    )


def main_kernel(
    nb, nt, span, gp, digits, window,
    depth_in, rough_in, seed_in, label_hbm, owner_hbm, keep_hbm, force_hbm, cell_hbm,
    packed_out,
    label_in, owner_in, keep_in, force_in, cell_in, ext, table, owner_f, slot_tab, cells, pieces, packed, home_sums, home_parts, diff_e, diff_s, adj_f,
    adj0, levee, hist, sums, pair, part, recv2, maps,
    halo_send, halo_recv, map_send, map_recv, one_send, one_recv, two_send, two_recv, load_sem,
):
    b = lax.axis_index("basin")
    t = lax.axis_index("tile")
    rows, cols = depth_in.shape
    label_groups = table.shape[1] // (1 + digits)
    groups = nb * nt * gp

    half = ROWS_AT_ONCE // 2
    blocks = nb * nt // 2
    side = lax.rem(t, 2)
    mine = b * (nt // 2) + t // 2

    def peer(k):
        other = lax.rem(mine + k, blocks)
        return other, (other // (nt // 2), 2 * lax.rem(other, nt // 2) + side)

    fields = (depth_in, rough_in, seed_in)
    pairs = (
        (depth_in, ext.at[0, pl.ds(HALO, rows)]), (rough_in, ext.at[1, pl.ds(HALO, rows)]),
        (seed_in, ext.at[2, pl.ds(HALO, rows)]),
        (owner_hbm, owner_in), (label_hbm, label_in),
        (cell_hbm, cell_in), (keep_hbm, keep_in), (force_hbm, force_in),
    )
    loads = [
        pltpu.make_async_copy(source, target, load_sem.at[index])
        for index, (source, target) in enumerate(pairs)
    ]
    for load in loads:
        load.start()
    barrier = pltpu.get_barrier_semaphore()
    for k in range(1, blocks):
        pl.semaphore_signal(barrier, inc=1, device_id=peer(k)[1], device_id_type=MESH)
    near = sorted({1, nt - 1})
    for k in near:
        pl.semaphore_signal(
            barrier, inc=1, device_id=(b, lax.rem(t + k, nt)), device_id_type=MESH
        )

    def down_copy(f):
        return pltpu.make_async_remote_copy(
            src_ref=fields[f].at[pl.ds(rows - HALO, HALO)],
            dst_ref=ext.at[f, pl.ds(0, HALO)],
            send_sem=halo_send.at[0, f],
            recv_sem=halo_recv.at[0, f],
            device_id=(b, lax.rem(t + 1, nt)),
            device_id_type=MESH,
        )

    def up_copy(f):
        return pltpu.make_async_remote_copy(
            src_ref=fields[f].at[pl.ds(0, HALO)],
            dst_ref=ext.at[f, pl.ds(HALO + rows, HALO)],
            send_sem=halo_send.at[1, f],
            recv_sem=halo_recv.at[1, f],
            device_id=(b, lax.rem(t + nt - 1, nt)),
            device_id_type=MESH,
        )

    def start_halos():
        @pl.when(t < nt - 1)
        def _():
            for f in range(3):
                down_copy(f).start()

        @pl.when(t > 0)
        def _():
            for f in range(3):
                up_copy(f).start()

    def right(v):
        return pltpu.roll(v, cols - 1, 1)

    def from_left(v):
        return pltpu.roll(v, 1, 1)

    def sweep(depth, rough, adjoint, mask_rows):
        deep = depth.shape[0]
        face_e = iota((deep, cols), 1) < cols - 1

        def below(v):
            return pltpu.roll(v, deep - 1, 0)

        def from_above(v):
            return pltpu.roll(v, 1, 0)

        conduct = rough_ref / rough
        inner = face_s = None
        if mask_rows is not None:
            inner, face_s = mask_rows
            conduct = jnp.where(inner, conduct, 0.0)
        weight_e = jnp.where(face_e, (0.5 * courant) * (conduct + right(conduct)), 0.0)
        weight_s = (0.5 * courant) * (conduct + below(conduct))
        if face_s is not None:
            weight_s = jnp.where(face_s, weight_s, 0.0)

        def advance(v, de, ds):
            flow_e = weight_e * de
            flow_s = weight_s * ds
            return v + ((flow_e - from_left(flow_e)) + (flow_s - from_above(flow_s)))

        for s in range(STEPS):
            de = right(depth) - depth
            ds = below(depth) - depth
            diff_e[s, pl.ds(0, deep)] = de
            diff_s[s, pl.ds(0, deep)] = ds
            if s < STEPS - 1:
                depth = advance(depth, de, ds)
        prod_e = jnp.zeros((deep, cols), F32)
        prod_s = jnp.zeros((deep, cols), F32)
        for s in reversed(range(STEPS)):
            de = right(adjoint) - adjoint
            ds = below(adjoint) - adjoint
            prod_e = prod_e + diff_e[s, pl.ds(0, deep)] * de
            prod_s = prod_s + diff_s[s, pl.ds(0, deep)] * ds
            adjoint = advance(adjoint, de, ds)
        prod_e = jnp.where(face_e, prod_e, 0.0)
        if face_s is not None:
            prod_s = jnp.where(face_s, prod_s, 0.0)
        product = (prod_e + from_left(prod_e)) + (prod_s + from_above(prod_s))
        gradient = (0.5 * courant) * conduct * product
        square = gradient * gradient
        parts = []
        for value in (gradient, square):
            high = value.astype(BF16).astype(F32)
            parts += [high, value - high]
        return parts, adjoint

    def interior():
        parts, adjoint = sweep(*(ext[f, pl.ds(HALO, rows)] for f in range(3)), None)
        for index, value in enumerate(parts):
            pieces[index] = pltpu.roll(value, rows - half, 0)
        adj_f[...] = adjoint

    def take_halos():
        @pl.when(t < nt - 1)
        def _():
            for f in range(3):
                down_copy(f).wait_send()
                up_copy(f).wait_recv()

        @pl.when(t > 0)
        def _():
            for f in range(3):
                up_copy(f).wait_send()
                down_copy(f).wait_recv()

        @pl.when(t == 0)
        def _():
            for f in range(3):
                ext[f, pl.ds(0, HALO)] = jnp.ones((HALO, cols), F32)

        @pl.when(t == nt - 1)
        def _():
            for f in range(3):
                ext[f, pl.ds(HALO + rows, HALO)] = jnp.ones((HALO, cols), F32)

    def edges():
        strip = 2 * HALO
        local = iota((2 * strip, cols), 0)
        row_id = jnp.where(local < strip, local, local + (rows - strip))
        first = jnp.where(t == 0, HALO, 0)
        last = jnp.where(t == nt - 1, HALO + rows - 1, rows + 2 * HALO - 1)
        masks = (
            (row_id >= first) & (row_id <= last), (row_id >= first) & (row_id < last)
        )
        parts, adjoint = sweep(
            *(
                jnp.concatenate([ext[f, pl.ds(0, strip)], ext[f, pl.ds(rows, strip)]], axis=0)
                for f in range(3)
            ),
            masks,
        )
        low = strip + HALO - STEPS
        for index, value in enumerate(parts):
            pieces[index, pl.ds(rows - ROWS_AT_ONCE, ROWS_AT_ONCE)] = jnp.concatenate(
                [value[low : low + half], value[HALO : HALO + half]], axis=0
            )
        adj_f[pl.ds(0, STEPS)] = adjoint[HALO : HALO + STEPS]
        adj_f[pl.ds(rows - STEPS, STEPS)] = adjoint[low : low + STEPS]
    for load in loads[:5]:
        load.wait()
    interior()
    owner = owner_in[...].astype(F32)
    device = jnp.floor((owner + 0.5) * (1.0 / span))
    inside = owner - device * span
    block = jnp.floor(inside * (1.0 / LANES))
    group = device * gp + block
    lane = inside - block * LANES
    owner_f[...] = jnp.zeros(owner_f.shape, F32)
    slot_tab[...] = jnp.zeros(slot_tab.shape, F32)
    held = owner.shape[0]
    slot_tab[pl.ds(0, held)] = group * LANES + lane
    parts = [lane]
    for digit in range(digits):
        upper = jnp.floor(group * (1.0 / 256.0))
        parts.append((group - upper * 256.0) * float(LANES * 256**digit))
        group = upper
    for index, value in enumerate(parts):
        owner_f[pl.ds(0, held)] = value
        table[:, pl.ds(index * label_groups, label_groups)] = owner_f[...].T.astype(BF16)
    count = iota((256, LANES), 0).astype(F32).astype(BF16)

    def spread_rows(row, size):
        tall = jnp.broadcast_to(row, (16, LANES)).astype(BF16)
        return tall if size == 16 else jnp.concatenate([tall] * (size // 16), axis=0)

    def row_of(ref, row):
        return ref[pl.ds(row, 1), :]

    def hot_rows(size, index):
        if size > 256:
            return jnp.where(iota((size, LANES), 0) == index.astype(I32), 1.0, 0.0).astype(BF16)
        return jnp.where(count[:size] == spread_rows(index, size), BF16(1), BF16(0))

    def side_by_side(pieces_of_row):
        return jnp.concatenate(pieces_of_row, axis=1)

    def split_dot(left, right, ways):
        step = -(-len(left) // ways)
        return sum(
            nt_dot(side_by_side(left[k : k + step]), side_by_side(right[k : k + step]))
            for k in range(0, len(left), step)
        )

    dev = b * nt + t
    first_group = (dev * span) // LANES
    home_rows = round_up(window, 16)
    per_group = 2 if cols % (2 * LANES) == 0 else 1
    places = LANES * LANES * per_group // cols

    def prepare():
        labels = pltpu.roll(label_in[...], rows - half, 0)
        group_of = lax.shift_right_logical(labels, 7)
        place = group_of - first_group
        stray = (place < 0) | (place >= window)
        wide = per_group * LANES
        before = jnp.where(iota((wide, wide), 0) <= iota((wide, wide), 1), 1.0, 0.0).astype(BF16)
        odd = jnp.where(stray, 1.0, 0.0).astype(BF16)
        rank = side_by_side(
            [
                jnp.dot(odd[:, k : k + wide], before, preferred_element_type=F32)
                for k in range(0, cols, wide)
            ]
        )
        cells[0] = group_of.astype(F32)
        cells[1] = jnp.bitwise_and(labels, LANES - 1).astype(F32)
        cells[2] = jnp.where(stray, -1.0, place.astype(F32))
        cells[3] = jnp.where(stray, rank - 1.0, -1.0)
        most = jnp.max(jnp.max(rank, axis=0, keepdims=True), axis=1, keepdims=True)
        over = jnp.where(most > places, 1.0, 0.0)
        hist[...] = jnp.zeros(hist.shape, F32)
        spare = (lax.rem(iota((groups, LANES), 0), gp) == gp - 1) & (
            iota((groups, LANES), 1) == LANES - 1
        )
        hist[:, pl.ds(0, LANES)] = jnp.where(spare, over, 0.0)
        home_sums[...] = jnp.zeros(home_sums.shape, F32)

    def compact(base, size):
        block = pl.ds(base, size)
        carried = [cells[i, block, :] for i in range(2)] + [pieces[i, block, :] for i in range(4)]
        carried.append(jnp.zeros((LANES - 6 * size, cols), F32))
        table_of_cells = jnp.concatenate(carried, axis=0).T.astype(BF16)
        home_left, home_right = [], []
        hot = [[] for _ in range(0, cols, per_group * LANES)]
        for q in range(size):
            labels = [cells[i, pl.ds(base + q, 1), :] for i in range(1, 4)]
            amounts = [pieces[i, pl.ds(base + q, 1), :] for i in range(4)]
            rows_of_hot = []
            for c in range(0, cols, LANES):
                lower, place, position = (v[:, c : c + LANES] for v in labels)
                values = [spread_rows(v[:, c : c + LANES], 16) for v in amounts]
                rows_of_hot.append(hot_rows(places, position))
                home_right.append(hot_rows(LANES, lower))
                weighted = []
                for first_row in range(0, home_rows, 16):
                    mask = count[first_row : first_row + 16] == spread_rows(place, 16)
                    weighted.append([jnp.where(mask, value, BF16(0)) for value in values])
                home_left.append(
                    jnp.concatenate([part_of[i] for i in range(4) for part_of in weighted], axis=0)
                )
            for k, group in enumerate(hot):
                group.append(side_by_side(rows_of_hot[k * per_group : (k + 1) * per_group]))
        lane_of = lax.rem(iota((places, LANES), 1), size)
        chosen = []
        for k, group in enumerate(hot):
            wide = per_group * LANES
            found = jnp.dot(
                jnp.concatenate(group, axis=0), table_of_cells[k * wide : (k + 1) * wide],
                preferred_element_type=F32,
            )
            total = jnp.zeros((places, LANES), F32)
            for q in range(size):
                total = jnp.where(lane_of == q, found[q * places : (q + 1) * places], total)
            chosen.append(total)
        packed[...] = jnp.concatenate(chosen, axis=0).T
        home_sums[...] += split_dot(home_right, home_left, 2)

    def add_to_slots(slots, values_of):
        hot_groups = []
        weighted = []
        for slot, values in zip(slots, values_of):
            index = slot.astype(I32)
            hot_groups.append(hot_rows(groups, lax.shift_right_logical(index, 7).astype(F32)))
            lane_row = jnp.bitwise_and(index, LANES - 1).astype(F32)
            mask = count[:LANES] == spread_rows(lane_row, LANES)
            weighted.append(
                jnp.concatenate(
                    [jnp.where(mask, spread_rows(v, LANES), BF16(0)) for v in values], axis=0
                )
            )
        hist[...] += nt_dot(side_by_side(hot_groups), side_by_side(weighted))

    def stray_sums(size):
        hot = side_by_side([hot_rows(label_groups, row_of(packed, q)) for q in range(size)])
        found = jnp.dot(
            table[...], jnp.concatenate([hot] * (1 + digits), axis=0), preferred_element_type=F32
        )
        slots = []
        for q in range(size):
            mask = iota((LANES, LANES), 0) == row_of(packed, size + q).astype(I32)
            slots.append(
                jnp.sum(
                    jnp.where(mask, found[:, q * LANES : (q + 1) * LANES], 0.0),
                    axis=0, keepdims=True,
                )
            )
        return slots, [[row_of(packed, (2 + i) * size + q) for i in range(4)] for q in range(size)]

    def home_totals():
        homes_t = home_sums[...].T
        for which in range(2):
            low = 2 * which * home_rows
            value = (homes_t[low : low + home_rows] + homes_t[low + home_rows : low + 2 * home_rows])
            high = value.astype(BF16).astype(F32)
            home_parts[2 * which] = high
            home_parts[2 * which + 1] = value - high
        return (
            [row_of(slot_tab, first_group + i) for i in range(window)],
            [[home_parts[k, pl.ds(i, 1), :] for k in range(4)] for i in range(window)],
        )

    chunks = rows // ROWS_AT_ONCE

    def inner_chunk(chunk, unused):
        add_to_slots(*stray_sums(BATCH))
        compact(chunk * BATCH if isinstance(chunk, int) else pl.multiple_of(chunk * BATCH, 8), BATCH)
        return unused

    prepare()
    steps = (rows - ROWS_AT_ONCE) // BATCH
    early = min(EARLY, steps)
    compact(0, BATCH)
    lax.fori_loop(1, early, inner_chunk, 0)
    pl.semaphore_wait(barrier, blocks - 1 + len(near))
    start_halos()
    lax.fori_loop(early, steps, inner_chunk, 0)
    held_rows = BATCH
    for base in range(steps * BATCH, rows - ROWS_AT_ONCE, ROWS_AT_ONCE):
        add_to_slots(*stray_sums(held_rows))
        compact(base, ROWS_AT_ONCE)
        held_rows = ROWS_AT_ONCE
    for load in loads[5:]:
        load.wait()

    def pair_copy():
        return pltpu.make_async_remote_copy(
            src_ref=sums.at[1 - side],
            dst_ref=pair,
            send_sem=one_send,
            recv_sem=one_recv,
            device_id=(b, t + 1 - 2 * side),
            device_id_type=MESH,
        )

    def two_copy(k):
        other, device = peer(k)
        return pltpu.make_async_remote_copy(
            src_ref=part.at[other],
            dst_ref=recv2.at[k - 1],
            send_sem=two_send.at[k - 1],
            recv_sem=two_recv.at[k - 1],
            device_id=device,
            device_id_type=MESH,
        )

    take_halos()
    add_to_slots(*stray_sums(held_rows))
    edges()
    compact(rows - ROWS_AT_ONCE, ROWS_AT_ONCE)
    strays, homes = stray_sums(ROWS_AT_ONCE), home_totals()
    add_to_slots(strays[0] + homes[0], strays[1] + homes[1])
    for which in range(2):
        low = 2 * which * LANES
        total = hist[:, pl.ds(low, LANES)] + hist[:, pl.ds(low + LANES, LANES)]
        total = total.reshape(blocks, 2, gp, LANES)
        for p in range(2):
            sums[p, :, which] = total[:, p]
    pair_copy().start()
    rest = adj_f[...]
    for piece in range(3):
        high = rest.astype(BF16)
        adj0[pl.ds(piece * rows, rows)] = high
        rest = rest - high.astype(F32)
    pair_copy().wait()
    part[...] = sums[side] + pair[...]
    for k in range(1, blocks):
        two_copy(k).start()
    reaches, chains = cell_in.shape
    shift = cols.bit_length() - 1

    def levees(chunk, unused):
        base = chunk * 4
        cells = jnp.concatenate([row_of(cell_in, base + q) for q in range(4)], axis=1)
        wide = 4 * chains
        column = jnp.bitwise_and(cells, cols - 1)
        line = lax.shift_right_logical(cells, shift)
        hot = jnp.where(iota((cols, wide), 0) == column, 1.0, 0.0).astype(BF16)
        picked = jnp.dot(adj0[...], hot, preferred_element_type=F32)
        picked = (picked[:rows] + picked[rows : 2 * rows]) + picked[2 * rows :]
        value = jnp.sum(
            jnp.where(iota((rows, wide), 0) == line, picked, 0.0), axis=0, keepdims=True
        )
        for q in range(4):
            levee[pl.ds(base + q, 1), :] = value[:, q * chains : (q + 1) * chains]
        return unused

    lax.fori_loop(0, reaches // 4, levees, 0)

    rate = keep_in[...]
    push = force_in[...] + levee_gain * levee[...]
    reach_id = iota((reaches, chains), 0)
    step = 1
    while step < reaches:
        has = reach_id < reaches - step
        next_rate = jnp.where(has, pltpu.roll(rate, reaches - step, 0), 1.0)
        next_push = jnp.where(has, pltpu.roll(push, reaches - step, 0), 0.0)
        push = push + rate * next_push
        rate = rate * next_rate
        step *= 2
    maps[0, pl.ds(0, 1)] = rate[0:1]
    maps[0, pl.ds(1, 1)] = push[0:1]
    maps[0, pl.ds(2, 6)] = jnp.zeros((6, chains), F32)

    def map_copy(k):
        return pltpu.make_async_remote_copy(
            src_ref=maps.at[0],
            dst_ref=maps.at[k],
            send_sem=map_send.at[k - 1],
            recv_sem=map_recv.at[k - 1],
            device_id=(lax.rem(b + k, nb), t),
            device_id_type=MESH,
        )

    for k in range(1, nb):
        map_copy(k).start()

    for k in range(1, nb):
        map_copy(k).wait()
    incoming = jnp.zeros((1, chains), F32)
    for other in reversed(range(nb)):
        slot = lax.rem(b - other + nb, nb)
        stretch = maps[slot]
        incoming = jnp.where(
            other > b, stretch[0:1] * incoming + stretch[1:2], incoming
        )
    packed_out[pl.ds(2 * gp, reaches)] = rate * incoming + push
    for k in range(1, blocks):
        two_copy(k).wait()
    total = part[mine]
    for k in range(1, blocks):
        total = total + recv2[k - 1]
    for which in range(2):
        packed_out[pl.ds(which * gp, gp)] = total[which]


def full_kernel(
    nb, nt, span, gp, digits,
    depth_in, rough_in, seed_in, label_hbm, owner_hbm, keep_hbm, force_hbm, cell_hbm,
    packed_out,
    label_in, owner_in, keep_in, force_in, cell_in, ext, table, owner_f, slot_s, pieces, diff_e, diff_s, adj0, levee,
    hist, sums, recv1, part, recv2, maps,
    halo_send, halo_recv, map_send, map_recv, one_send, one_recv, two_send, two_recv, load_sem,
):
    b = lax.axis_index("basin")
    t = lax.axis_index("tile")
    rows, cols = depth_in.shape
    label_groups = table.shape[1] // (1 + digits)
    groups = nb * nt * gp

    barrier = pltpu.get_barrier_semaphore()
    for k in range(1, nb):
        pl.semaphore_signal(
            barrier, inc=1, device_id=(lax.rem(b + k, nb), t), device_id_type=MESH
        )
    for k in range(1, nt):
        pl.semaphore_signal(
            barrier, inc=1, device_id=(b, lax.rem(t + k, nt)), device_id_type=MESH
        )

    fields = (depth_in, rough_in, seed_in)
    pairs = (
        (owner_hbm, owner_in), (label_hbm, label_in),
        (depth_in, ext.at[0, pl.ds(HALO, rows)]), (rough_in, ext.at[1, pl.ds(HALO, rows)]),
        (seed_in, ext.at[2, pl.ds(HALO, rows)]),
        (cell_hbm, cell_in), (keep_hbm, keep_in), (force_hbm, force_in),
    )
    loads = [
        pltpu.make_async_copy(source, target, load_sem.at[index])
        for index, (source, target) in enumerate(pairs)
    ]
    for load in loads:
        load.start()
    pl.semaphore_wait(barrier, nb - 1 + nt - 1)

    def down_copy(f):
        return pltpu.make_async_remote_copy(
            src_ref=fields[f].at[pl.ds(rows - HALO, HALO)],
            dst_ref=ext.at[f, pl.ds(0, HALO)],
            send_sem=halo_send.at[0, f],
            recv_sem=halo_recv.at[0, f],
            device_id=(b, lax.rem(t + 1, nt)),
            device_id_type=MESH,
        )

    def up_copy(f):
        return pltpu.make_async_remote_copy(
            src_ref=fields[f].at[pl.ds(0, HALO)],
            dst_ref=ext.at[f, pl.ds(HALO + rows, HALO)],
            send_sem=halo_send.at[1, f],
            recv_sem=halo_recv.at[1, f],
            device_id=(b, lax.rem(t + nt - 1, nt)),
            device_id_type=MESH,
        )

    @pl.when(t < nt - 1)
    def _():
        for f in range(3):
            down_copy(f).start()

    @pl.when(t > 0)
    def _():
        for f in range(3):
            up_copy(f).start()

    loads[0].wait()
    owner = owner_in[...].astype(F32)
    device = jnp.floor((owner + 0.5) * (1.0 / span))
    inside = owner - device * span
    block = jnp.floor(inside * (1.0 / LANES))
    group = device * gp + block
    lane = inside - block * LANES
    owner_f[...] = jnp.zeros(owner_f.shape, F32)
    held = owner.shape[0]
    parts = [lane]
    for digit in range(digits):
        upper = jnp.floor(group * (1.0 / 256.0))
        parts.append((group - upper * 256.0) * float(LANES * 256**digit))
        group = upper
    for index, value in enumerate(parts):
        owner_f[pl.ds(0, held)] = value
        table[:, pl.ds(index * label_groups, label_groups)] = owner_f[...].T.astype(BF16)
    count = iota((256, LANES), 0).astype(F32).astype(BF16)

    def spread_rows(row, size):
        tall = jnp.broadcast_to(row, (16, LANES)).astype(BF16)
        return jnp.concatenate([tall] * (size // 16), axis=0)

    def row_of(ref, row):
        return ref[pl.ds(row, 1), :]

    def hot_rows(size, index):
        if size > 256:
            return jnp.where(iota((size, cols), 0) == index, 1.0, 0.0).astype(BF16)
        narrow = index.astype(F32)
        return jnp.concatenate(
            [
                jnp.where(
                    count[:size] == spread_rows(narrow[:, c : c + LANES], size), BF16(1), BF16(0)
                )
                for c in range(0, cols, LANES)
            ],
            axis=1,
        )

    def look_up(chunk, unused):
        for q in range(ROWS_AT_ONCE):
            row = chunk * ROWS_AT_ONCE + q
            labels = row_of(label_in, row)
            hot = hot_rows(label_groups, lax.shift_right_logical(labels, 7))
            found = jnp.dot(
                table[...],
                jnp.concatenate([hot] * (1 + digits), axis=0),
                preferred_element_type=F32,
            )
            mask = iota((LANES, cols), 0) == jnp.bitwise_and(labels, LANES - 1)
            slot_s[pl.ds(row, 1), :] = jnp.sum(
                jnp.where(mask, found, 0.0), axis=0, keepdims=True
            )
        return unused

    loads[1].wait()
    lax.fori_loop(0, rows // ROWS_AT_ONCE, look_up, 0)
    for load in loads[2:]:
        load.wait()

    @pl.when(t < nt - 1)
    def _():
        for f in range(3):
            down_copy(f).wait_send()
            up_copy(f).wait_recv()

    @pl.when(t > 0)
    def _():
        for f in range(3):
            up_copy(f).wait_send()
            down_copy(f).wait_recv()

    @pl.when(t == 0)
    def _():
        for f in range(3):
            ext[f, pl.ds(0, HALO)] = jnp.ones((HALO, cols), F32)

    @pl.when(t == nt - 1)
    def _():
        for f in range(3):
            ext[f, pl.ds(HALO + rows, HALO)] = jnp.ones((HALO, cols), F32)

    deep = rows + 2 * HALO
    row_id = iota((deep, cols), 0)
    col_id = iota((deep, cols), 1)
    first = jnp.where(t == 0, HALO, 0)
    last = jnp.where(t == nt - 1, HALO + rows - 1, deep - 1)
    inner = (row_id >= first) & (row_id <= last)
    face_s = (row_id >= first) & (row_id < last)
    face_e = col_id < cols - 1

    def below(v):
        return pltpu.roll(v, deep - 1, 0)

    def right(v):
        return pltpu.roll(v, cols - 1, 1)

    def from_above(v):
        return pltpu.roll(v, 1, 0)

    def from_left(v):
        return pltpu.roll(v, 1, 1)

    conduct = jnp.where(inner, rough_ref / ext[1], 0.0)
    weight_e = jnp.where(face_e, (0.5 * courant) * (conduct + right(conduct)), 0.0)
    weight_s = jnp.where(face_s, (0.5 * courant) * (conduct + below(conduct)), 0.0)

    def advance(v, de, ds):
        flow_e = weight_e * de
        flow_s = weight_s * ds
        return v + ((flow_e - from_left(flow_e)) + (flow_s - from_above(flow_s)))

    depth = ext[0]
    for s in range(STEPS):
        de = right(depth) - depth
        ds = below(depth) - depth
        diff_e[s] = de
        diff_s[s] = ds
        if s < STEPS - 1:
            depth = advance(depth, de, ds)
    adjoint = ext[2]
    prod_e = jnp.zeros((deep, cols), F32)
    prod_s = jnp.zeros((deep, cols), F32)
    for s in reversed(range(STEPS)):
        de = right(adjoint) - adjoint
        ds = below(adjoint) - adjoint
        prod_e = prod_e + diff_e[s] * de
        prod_s = prod_s + diff_s[s] * ds
        adjoint = advance(adjoint, de, ds)
    prod_e = jnp.where(face_e, prod_e, 0.0)
    prod_s = jnp.where(face_s, prod_s, 0.0)
    product = (prod_e + from_left(prod_e)) + (prod_s + from_above(prod_s))
    gradient = ((0.5 * courant) * conduct * product)[HALO : HALO + rows]
    square = gradient * gradient
    for index, value in enumerate((gradient, square)):
        high = value.astype(BF16).astype(F32)
        pieces[2 * index] = high
        pieces[2 * index + 1] = value - high

    def gather_rows(which, chunk, unused):
        hot_groups = []
        weighted = []
        for q in range(ROWS_AT_ONCE):
            row = chunk * ROWS_AT_ONCE + q
            slot = row_of(slot_s, row).astype(I32)
            hot_groups.append(hot_rows(groups, lax.shift_right_logical(slot, 7)))
            lane_row = jnp.bitwise_and(slot, LANES - 1).astype(F32)
            values = [pieces[i, pl.ds(row, 1), :] for i in range(4)]
            masked = []
            for c in range(0, cols, LANES):
                mask = count[:LANES] == spread_rows(lane_row[:, c : c + LANES], LANES)
                masked.append(
                    jnp.concatenate(
                        [
                            jnp.where(mask, spread_rows(v[:, c : c + LANES], LANES), BF16(0))
                            for v in values
                        ],
                        axis=0,
                    )
                )
            weighted.append(jnp.concatenate(masked, axis=1))
        hist[...] += nt_dot(
            jnp.concatenate(weighted, axis=1), jnp.concatenate(hot_groups, axis=1)
        )
        return unused

    chunks = rows // ROWS_AT_ONCE

    def one_copy(which, k):
        other = lax.rem(b + k, nb)
        return pltpu.make_async_remote_copy(
            src_ref=sums.at[which, pl.ds(pl.multiple_of(other * (nt * gp), 8), nt * gp)],
            dst_ref=recv1.at[k - 1, which],
            send_sem=one_send.at[which, k - 1],
            recv_sem=one_recv.at[which, k - 1],
            device_id=(other, t),
            device_id_type=MESH,
        )

    def two_copy(which, k):
        other = lax.rem(t + k, nt)
        return pltpu.make_async_remote_copy(
            src_ref=part.at[which, pl.ds(pl.multiple_of(other * gp, 8), gp)],
            dst_ref=recv2.at[k - 1, which],
            send_sem=two_send.at[which, k - 1],
            recv_sem=two_recv.at[which, k - 1],
            device_id=(b, other),
            device_id_type=MESH,
        )

    def collect(which, start, stop):
        lax.fori_loop(start, stop, functools.partial(gather_rows, which), 0)

    def first_phase(which):
        sums[which] = (hist[pl.ds(2 * which * LANES, LANES)] + hist[pl.ds((2 * which + 1) * LANES, LANES)]).T
        for k in range(1, nb):
            one_copy(which, k).start()

    def second_phase(which):
        for k in range(1, nb):
            one_copy(which, k).wait()
        total = sums[which, pl.ds(pl.multiple_of(b * (nt * gp), 8), nt * gp)]
        for k in range(1, nb):
            total = total + recv1[k - 1, which]
        part[which] = total
        for k in range(1, nt):
            two_copy(which, k).start()

    def finish(which):
        for k in range(1, nt):
            two_copy(which, k).wait()
        total = part[which, pl.ds(pl.multiple_of(t * gp, 8), gp)]
        for k in range(1, nt):
            total = total + recv2[k - 1, which]
        packed_out[pl.ds(which * gp, gp)] = total

    hist[...] = jnp.zeros(hist.shape, F32)
    collect(0, 0, chunks)
    first_phase(0)
    first_phase(1)
    rest = adjoint[HALO : HALO + rows]
    for piece in range(3):
        high = rest.astype(BF16)
        adj0[pl.ds(piece * rows, rows)] = high
        rest = rest - high.astype(F32)
    reaches, chains = cell_in.shape
    shift = cols.bit_length() - 1

    def levees(chunk, unused):
        base = chunk * 4
        cells = jnp.concatenate([row_of(cell_in, base + q) for q in range(4)], axis=1)
        wide = 4 * chains
        column = jnp.bitwise_and(cells, cols - 1)
        line = lax.shift_right_logical(cells, shift)
        hot = jnp.where(iota((cols, wide), 0) == column, 1.0, 0.0).astype(BF16)
        picked = jnp.dot(adj0[...], hot, preferred_element_type=F32)
        picked = (picked[:rows] + picked[rows : 2 * rows]) + picked[2 * rows :]
        value = jnp.sum(
            jnp.where(iota((rows, wide), 0) == line, picked, 0.0), axis=0, keepdims=True
        )
        for q in range(4):
            levee[pl.ds(base + q, 1), :] = value[:, q * chains : (q + 1) * chains]
        return unused

    lax.fori_loop(0, reaches // 4, levees, 0)

    rate = keep_in[...]
    push = force_in[...] + levee_gain * levee[...]
    reach_id = iota((reaches, chains), 0)
    step = 1
    while step < reaches:
        has = reach_id < reaches - step
        next_rate = jnp.where(has, pltpu.roll(rate, reaches - step, 0), 1.0)
        next_push = jnp.where(has, pltpu.roll(push, reaches - step, 0), 0.0)
        push = push + rate * next_push
        rate = rate * next_rate
        step *= 2
    maps[0, pl.ds(0, 1)] = rate[0:1]
    maps[0, pl.ds(1, 1)] = push[0:1]
    maps[0, pl.ds(2, 6)] = jnp.zeros((6, chains), F32)

    def map_copy(k):
        return pltpu.make_async_remote_copy(
            src_ref=maps.at[0],
            dst_ref=maps.at[k],
            send_sem=map_send.at[k - 1],
            recv_sem=map_recv.at[k - 1],
            device_id=(lax.rem(b + k, nb), t),
            device_id_type=MESH,
        )

    for k in range(1, nb):
        map_copy(k).start()

    second_phase(0)
    second_phase(1)
    for k in range(1, nb):
        map_copy(k).wait()
    incoming = jnp.zeros((1, chains), F32)
    for other in reversed(range(nb)):
        slot = lax.rem(b - other + nb, nb)
        stretch = maps[slot]
        incoming = jnp.where(
            other > b, stretch[0:1] * incoming + stretch[1:2], incoming
        )
    packed_out[pl.ds(2 * gp, reaches)] = rate * incoming + push
    finish(0)
    finish(1)


def unpack(gp, packed_in, grad_out, curv_out, reach_out):
    grad_out[...] = packed_in[pl.ds(0, gp)]
    curv_out[...] = packed_in[pl.ds(gp, gp)]
    reach_out[...] = packed_in[pl.ds(2 * gp, reach_out.shape[0])]


def full_pass(
    nb, nt, gp, depth_start, roughness, depth_seed, zone_label, owner_slot, retention, forcing,
    levee_cell,
):
    zones = owner_slot.shape[0]
    span = zones // (nb * nt)
    groups = nb * nt * gp
    digits = 1 if groups <= 256 else 2
    rows, cols = depth_start.shape[1:]
    reaches, chains = retention.shape
    padded = round_up(zones, LANES)
    owner = jnp.pad(owner_slot, (0, padded - zones)).reshape(-1, LANES)
    label_groups = round_up(owner.shape[0], LANES)
    deep = rows + 2 * HALO
    vmem = pl.BlockSpec(memory_space=pltpu.VMEM)
    dma = pltpu.SemaphoreType.DMA
    return pl.pallas_call(
        functools.partial(full_kernel, nb, nt, span, gp, digits),
        out_shape=jax.ShapeDtypeStruct((2 * gp + reaches, LANES), F32),
        in_specs=[pl.BlockSpec(memory_space=pl.ANY)] * 8,
        out_specs=vmem,
        scratch_shapes=[
            pltpu.VMEM((rows, cols), I32),
            pltpu.VMEM(owner.shape, I32),
            pltpu.VMEM((reaches, chains), F32),
            pltpu.VMEM((reaches, chains), F32),
            pltpu.VMEM((reaches, chains), I32),
            pltpu.VMEM((3, deep, cols), F32),
            pltpu.VMEM((LANES, (1 + digits) * label_groups), BF16),
            pltpu.VMEM((label_groups, LANES), F32),
            pltpu.VMEM((rows, cols), F32),
            pltpu.VMEM((4, rows, cols), F32),
            pltpu.VMEM((STEPS, deep, cols), F32),
            pltpu.VMEM((STEPS, deep, cols), F32),
            pltpu.VMEM((3 * rows, cols), BF16),
            pltpu.VMEM((reaches, chains), F32),
            pltpu.VMEM((4 * LANES, groups), F32),
            pltpu.VMEM((2, groups, LANES), F32),
            pltpu.VMEM((nb - 1, 2, nt * gp, LANES), F32),
            pltpu.VMEM((2, nt * gp, LANES), F32),
            pltpu.VMEM((nt - 1, 2, gp, LANES), F32),
            pltpu.VMEM((nb, 8, chains), F32),
            dma((2, 3)), dma((2, 3)),
            dma((nb - 1,)), dma((nb - 1,)),
            dma((2, nb - 1)), dma((2, nb - 1)),
            dma((2, nt - 1)), dma((2, nt - 1)),
            dma((8,)),
        ],
        compiler_params=pltpu.CompilerParams(collective_id=1, has_side_effects=True),
    )(
        depth_start[0], roughness[0], depth_seed[0], zone_label[0], owner, retention, forcing,
        levee_cell,
    )


def per_device(
    nb, nt, depth_start, roughness, depth_seed, zone_label, owner_slot, retention, forcing,
    levee_cell,
):
    zones = owner_slot.shape[0]
    span = zones // (nb * nt)
    gp = round_up(round_up(span + 1, LANES) // LANES, 8)
    window = (span + LANES - 2) // LANES + 1
    home_rows = round_up(window, 16)
    groups = nb * nt * gp
    digits = 1 if groups <= 256 else 2
    blocks = nb * nt // 2
    rows, cols = depth_start.shape[1:]
    reaches, chains = retention.shape
    padded = round_up(zones, LANES)
    owner = jnp.pad(owner_slot, (0, padded - zones)).reshape(-1, LANES)
    label_groups = round_up(owner.shape[0], LANES)
    deep = rows + 2 * HALO
    vmem = pl.BlockSpec(memory_space=pltpu.VMEM)
    dma = pltpu.SemaphoreType.DMA
    packed = pl.pallas_call(
        functools.partial(main_kernel, nb, nt, span, gp, digits, window),
        out_shape=jax.ShapeDtypeStruct((2 * gp + reaches, LANES), F32),
        in_specs=[pl.BlockSpec(memory_space=pl.ANY)] * 8,
        out_specs=vmem,
        scratch_shapes=[
            pltpu.VMEM((rows, cols), I32),
            pltpu.VMEM(owner.shape, I32),
            pltpu.VMEM((reaches, chains), F32),
            pltpu.VMEM((reaches, chains), F32),
            pltpu.VMEM((reaches, chains), I32),
            pltpu.VMEM((3, deep, cols), F32),
            pltpu.VMEM((LANES, (1 + digits) * label_groups), BF16),
            pltpu.VMEM((label_groups, LANES), F32),
            pltpu.VMEM((label_groups + home_rows, LANES), F32),
            pltpu.VMEM((4, rows, cols), F32),
            pltpu.VMEM((4, rows, cols), F32),
            pltpu.VMEM((LANES, LANES), F32),
            pltpu.VMEM((LANES, 4 * home_rows), F32),
            pltpu.VMEM((4, home_rows, LANES), F32),
            pltpu.VMEM((STEPS, rows, cols), F32),
            pltpu.VMEM((STEPS, rows, cols), F32),
            pltpu.VMEM((rows, cols), F32),
            pltpu.VMEM((3 * rows, cols), BF16),
            pltpu.VMEM((reaches, chains), F32),
            pltpu.VMEM((groups, 4 * LANES), F32),
            pltpu.VMEM((2, blocks, 2, gp, LANES), F32),
            pltpu.VMEM((blocks, 2, gp, LANES), F32),
            pltpu.VMEM((blocks, 2, gp, LANES), F32),
            pltpu.VMEM((blocks - 1, 2, gp, LANES), F32),
            pltpu.VMEM((nb, 8, chains), F32),
            dma((2, 3)), dma((2, 3)),
            dma((nb - 1,)), dma((nb - 1,)),
            dma, dma,
            dma((blocks - 1,)), dma((blocks - 1,)),
            dma((8,)),
        ],
        compiler_params=pltpu.CompilerParams(collective_id=0, has_side_effects=True),
    )(
        depth_start[0], roughness[0], depth_seed[0], zone_label[0], owner, retention, forcing,
        levee_cell,
    )

    def unpack_with(words, value):
        return pl.pallas_call(
            functools.partial(unpack, words),
            out_shape=(
                jax.ShapeDtypeStruct((words, LANES), F32),
                jax.ShapeDtypeStruct((words, LANES), F32),
                jax.ShapeDtypeStruct((reaches, chains), F32),
            ),
            in_specs=[vmem],
            out_specs=(vmem,) * 3,
        )(value)

    def crowded(value):
        again = full_pass(
            nb, nt, gp, depth_start, roughness, depth_seed, zone_label, owner_slot, retention,
            forcing, levee_cell,
        )
        return unpack_with(gp, again)

    grad, curv, reach = lax.cond(
        packed[gp - 1, LANES - 1] > 0.5, crowded, functools.partial(unpack_with, gp), packed
    )
    return grad.reshape(-1)[:span], curv.reshape(-1)[:span], reach


def solution(mesh):
    in_specs = (
        P("basin", "tile", None),
        P("basin", "tile", None),
        P("basin", "tile", None),
        P("basin", "tile", None),
        P(),
        P("basin", "tile"),
        P("basin", "tile"),
        P("basin", "tile"),
    )
    out_specs = (P(("basin", "tile")), P(("basin", "tile")), P("basin", "tile"))
    return jax.shard_map(
        functools.partial(per_device, mesh.shape["basin"], mesh.shape["tile"]),
        mesh=mesh, in_specs=in_specs, out_specs=out_specs, check_vma=False,
    )
```

```python
import functools

import jax
import jax.numpy as jnp
from jax import lax
from jax.experimental import pallas as pl
from jax.experimental.pallas import tpu as pltpu
from jax.sharding import PartitionSpec as P

STEPS = 4
HALO = 8
LANES = 128
ROWS_AT_ONCE = 8
BATCH = 16
EARLY = 2

courant = 0.24
rough_ref = 0.025
levee_gain = 0.1

F32 = jnp.float32
BF16 = jnp.bfloat16
I32 = jnp.int32
MESH = pl.DeviceIdType.MESH


def round_up(value, unit):
    return -(-value // unit) * unit


def iota(shape, dim):
    return lax.broadcasted_iota(I32, shape, dim)


def nt_dot(left, right):
    return lax.dot_general(
        left, right, (((1,), (1,)), ((), ())), preferred_element_type=F32
    )


def main_kernel(
    nb, nt, span, gp, digits, window,
    depth_in, rough_in, seed_in, label_hbm, owner_hbm, keep_hbm, force_hbm, cell_hbm,
    packed_out,
    label_in, owner_in, keep_in, force_in, cell_in, ext, table, owner_f, slot_tab, cells, pieces, packed, home_sums, home_parts, diff_e, diff_s, adj_f,
    adj0, levee, hist, sums, pair, part, recv2, maps,
    halo_send, halo_recv, map_send, map_recv, one_send, one_recv, two_send, two_recv, load_sem,
):
    b = lax.axis_index("basin")
    t = lax.axis_index("tile")
    rows, cols = depth_in.shape
    label_groups = table.shape[1] // (1 + digits)
    groups = nb * nt * gp

    half = ROWS_AT_ONCE // 2
    blocks = nb * nt // 2
    side = lax.rem(t, 2)
    mine = b * (nt // 2) + t // 2

    def peer(k):
        other = lax.rem(mine + k, blocks)
        return other, (other // (nt // 2), 2 * lax.rem(other, nt // 2) + side)

    fields = (depth_in, rough_in, seed_in)
    pairs = (
        (depth_in, ext.at[0, pl.ds(HALO, rows)]), (rough_in, ext.at[1, pl.ds(HALO, rows)]),
        (seed_in, ext.at[2, pl.ds(HALO, rows)]),
        (owner_hbm, owner_in), (label_hbm, label_in),
        (cell_hbm, cell_in), (keep_hbm, keep_in), (force_hbm, force_in),
    )
    loads = [
        pltpu.make_async_copy(source, target, load_sem.at[index])
        for index, (source, target) in enumerate(pairs)
    ]
    for load in loads:
        load.start()
    barrier = pltpu.get_barrier_semaphore()
    for k in range(1, blocks):
        pl.semaphore_signal(barrier, inc=1, device_id=peer(k)[1], device_id_type=MESH)
    near = sorted({1, nt - 1})
    for k in near:
        pl.semaphore_signal(
            barrier, inc=1, device_id=(b, lax.rem(t + k, nt)), device_id_type=MESH
        )

    def down_copy(f):
        return pltpu.make_async_remote_copy(
            src_ref=fields[f].at[pl.ds(rows - HALO, HALO)],
            dst_ref=ext.at[f, pl.ds(0, HALO)],
            send_sem=halo_send.at[0, f],
            recv_sem=halo_recv.at[0, f],
            device_id=(b, lax.rem(t + 1, nt)),
            device_id_type=MESH,
        )

    def up_copy(f):
        return pltpu.make_async_remote_copy(
            src_ref=fields[f].at[pl.ds(0, HALO)],
            dst_ref=ext.at[f, pl.ds(HALO + rows, HALO)],
            send_sem=halo_send.at[1, f],
            recv_sem=halo_recv.at[1, f],
            device_id=(b, lax.rem(t + nt - 1, nt)),
            device_id_type=MESH,
        )

    def start_halos():
        @pl.when(t < nt - 1)
        def _():
            for f in range(3):
                down_copy(f).start()

        @pl.when(t > 0)
        def _():
            for f in range(3):
                up_copy(f).start()

    def right(v):
        return pltpu.roll(v, cols - 1, 1)

    def from_left(v):
        return pltpu.roll(v, 1, 1)

    def sweep(depth, rough, adjoint, mask_rows):
        deep = depth.shape[0]
        face_e = iota((deep, cols), 1) < cols - 1

        def below(v):
            return pltpu.roll(v, deep - 1, 0)

        def from_above(v):
            return pltpu.roll(v, 1, 0)

        conduct = rough_ref / rough
        inner = face_s = None
        if mask_rows is not None:
            inner, face_s = mask_rows
            conduct = jnp.where(inner, conduct, 0.0)
        weight_e = jnp.where(face_e, (0.5 * courant) * (conduct + right(conduct)), 0.0)
        weight_s = (0.5 * courant) * (conduct + below(conduct))
        if face_s is not None:
            weight_s = jnp.where(face_s, weight_s, 0.0)

        def advance(v, de, ds):
            flow_e = weight_e * de
            flow_s = weight_s * ds
            return v + ((flow_e - from_left(flow_e)) + (flow_s - from_above(flow_s)))

        for s in range(STEPS):
            de = right(depth) - depth
            ds = below(depth) - depth
            diff_e[s, pl.ds(0, deep)] = de
            diff_s[s, pl.ds(0, deep)] = ds
            if s < STEPS - 1:
                depth = advance(depth, de, ds)
        prod_e = jnp.zeros((deep, cols), F32)
        prod_s = jnp.zeros((deep, cols), F32)
        for s in reversed(range(STEPS)):
            de = right(adjoint) - adjoint
            ds = below(adjoint) - adjoint
            prod_e = prod_e + diff_e[s, pl.ds(0, deep)] * de
            prod_s = prod_s + diff_s[s, pl.ds(0, deep)] * ds
            adjoint = advance(adjoint, de, ds)
        prod_e = jnp.where(face_e, prod_e, 0.0)
        if face_s is not None:
            prod_s = jnp.where(face_s, prod_s, 0.0)
        product = (prod_e + from_left(prod_e)) + (prod_s + from_above(prod_s))
        gradient = (0.5 * courant) * conduct * product
        square = gradient * gradient
        parts = []
        for value in (gradient, square):
            high = value.astype(BF16).astype(F32)
            parts += [high, value - high]
        return parts, adjoint

    def interior():
        parts, adjoint = sweep(*(ext[f, pl.ds(HALO, rows)] for f in range(3)), None)
        for index, value in enumerate(parts):
            pieces[index] = pltpu.roll(value, rows - half, 0)
        adj_f[...] = adjoint

    def take_halos():
        @pl.when(t < nt - 1)
        def _():
            for f in range(3):
                down_copy(f).wait_send()
                up_copy(f).wait_recv()

        @pl.when(t > 0)
        def _():
            for f in range(3):
                up_copy(f).wait_send()
                down_copy(f).wait_recv()

        @pl.when(t == 0)
        def _():
            for f in range(3):
                ext[f, pl.ds(0, HALO)] = jnp.ones((HALO, cols), F32)

        @pl.when(t == nt - 1)
        def _():
            for f in range(3):
                ext[f, pl.ds(HALO + rows, HALO)] = jnp.ones((HALO, cols), F32)

    def edges():
        strip = 2 * HALO
        local = iota((2 * strip, cols), 0)
        row_id = jnp.where(local < strip, local, local + (rows - strip))
        first = jnp.where(t == 0, HALO, 0)
        last = jnp.where(t == nt - 1, HALO + rows - 1, rows + 2 * HALO - 1)
        masks = (
            (row_id >= first) & (row_id <= last), (row_id >= first) & (row_id < last)
        )
        parts, adjoint = sweep(
            *(
                jnp.concatenate([ext[f, pl.ds(0, strip)], ext[f, pl.ds(rows, strip)]], axis=0)
                for f in range(3)
            ),
            masks,
        )
        low = strip + HALO - STEPS
        for index, value in enumerate(parts):
            pieces[index, pl.ds(rows - ROWS_AT_ONCE, ROWS_AT_ONCE)] = jnp.concatenate(
                [value[low : low + half], value[HALO : HALO + half]], axis=0
            )
        adj_f[pl.ds(0, STEPS)] = adjoint[HALO : HALO + STEPS]
        adj_f[pl.ds(rows - STEPS, STEPS)] = adjoint[low : low + STEPS]
    for load in loads[:5]:
        load.wait()
    interior()
    owner = owner_in[...].astype(F32)
    device = jnp.floor((owner + 0.5) * (1.0 / span))
    inside = owner - device * span
    block = jnp.floor(inside * (1.0 / LANES))
    group = device * gp + block
    lane = inside - block * LANES
    owner_f[...] = jnp.zeros(owner_f.shape, F32)
    slot_tab[...] = jnp.zeros(slot_tab.shape, F32)
    held = owner.shape[0]
    slot_tab[pl.ds(0, held)] = group * LANES + lane
    parts = [lane]
    for digit in range(digits):
        upper = jnp.floor(group * (1.0 / 256.0))
        parts.append((group - upper * 256.0) * float(LANES * 256**digit))
        group = upper
    for index, value in enumerate(parts):
        owner_f[pl.ds(0, held)] = value
        table[:, pl.ds(index * label_groups, label_groups)] = owner_f[...].T.astype(BF16)
    count = iota((256, LANES), 0).astype(F32).astype(BF16)

    def spread_rows(row, size):
        tall = jnp.broadcast_to(row, (16, LANES)).astype(BF16)
        return tall if size == 16 else jnp.concatenate([tall] * (size // 16), axis=0)

    def row_of(ref, row):
        return ref[pl.ds(row, 1), :]

    def hot_rows(size, index):
        if size > 256:
            return jnp.where(iota((size, LANES), 0) == index.astype(I32), 1.0, 0.0).astype(BF16)
        return jnp.where(count[:size] == spread_rows(index, size), BF16(1), BF16(0))

    def side_by_side(pieces_of_row):
        return jnp.concatenate(pieces_of_row, axis=1)

    def split_dot(left, right, ways):
        step = -(-len(left) // ways)
        return sum(
            nt_dot(side_by_side(left[k : k + step]), side_by_side(right[k : k + step]))
            for k in range(0, len(left), step)
        )

    dev = b * nt + t
    first_group = (dev * span) // LANES
    home_rows = round_up(window, 16)
    per_group = 2 if cols % (2 * LANES) == 0 else 1
    places = LANES * LANES * per_group // cols

    def prepare():
        labels = pltpu.roll(label_in[...], rows - half, 0)
        group_of = lax.shift_right_logical(labels, 7)
        place = group_of - first_group
        stray = (place < 0) | (place >= window)
        wide = per_group * LANES
        before = jnp.where(iota((wide, wide), 0) <= iota((wide, wide), 1), 1.0, 0.0).astype(BF16)
        odd = jnp.where(stray, 1.0, 0.0).astype(BF16)
        rank = side_by_side(
            [
                jnp.dot(odd[:, k : k + wide], before, preferred_element_type=F32)
                for k in range(0, cols, wide)
            ]
        )
        cells[0] = group_of.astype(F32)
        cells[1] = jnp.bitwise_and(labels, LANES - 1).astype(F32)
        cells[2] = jnp.where(stray, -1.0, place.astype(F32))
        cells[3] = jnp.where(stray, rank - 1.0, -1.0)
        most = jnp.max(jnp.max(rank, axis=0, keepdims=True), axis=1, keepdims=True)
        over = jnp.where(most > places, 1.0, 0.0)
        hist[...] = jnp.zeros(hist.shape, F32)
        spare = (lax.rem(iota((groups, LANES), 0), gp) == gp - 1) & (
            iota((groups, LANES), 1) == LANES - 1
        )
        hist[:, pl.ds(0, LANES)] = jnp.where(spare, over, 0.0)
        home_sums[...] = jnp.zeros(home_sums.shape, F32)

    def compact(base, size):
        block = pl.ds(base, size)
        carried = [cells[i, block, :] for i in range(2)] + [pieces[i, block, :] for i in range(4)]
        carried.append(jnp.zeros((LANES - 6 * size, cols), F32))
        table_of_cells = jnp.concatenate(carried, axis=0).T.astype(BF16)
        home_left, home_right = [], []
        hot = [[] for _ in range(0, cols, per_group * LANES)]
        for q in range(size):
            labels = [cells[i, pl.ds(base + q, 1), :] for i in range(1, 4)]
            amounts = [pieces[i, pl.ds(base + q, 1), :] for i in range(4)]
            rows_of_hot = []
            for c in range(0, cols, LANES):
                lower, place, position = (v[:, c : c + LANES] for v in labels)
                values = [spread_rows(v[:, c : c + LANES], 16) for v in amounts]
                rows_of_hot.append(hot_rows(places, position))
                home_right.append(hot_rows(LANES, lower))
                weighted = []
                for first_row in range(0, home_rows, 16):
                    mask = count[first_row : first_row + 16] == spread_rows(place, 16)
                    weighted.append([jnp.where(mask, value, BF16(0)) for value in values])
                home_left.append(
                    jnp.concatenate([part_of[i] for i in range(4) for part_of in weighted], axis=0)
                )
            for k, group in enumerate(hot):
                group.append(side_by_side(rows_of_hot[k * per_group : (k + 1) * per_group]))
        lane_of = lax.rem(iota((places, LANES), 1), size)
        chosen = []
        for k, group in enumerate(hot):
            wide = per_group * LANES
            found = jnp.dot(
                jnp.concatenate(group, axis=0), table_of_cells[k * wide : (k + 1) * wide],
                preferred_element_type=F32,
            )
            total = jnp.zeros((places, LANES), F32)
            for q in range(size):
                total = jnp.where(lane_of == q, found[q * places : (q + 1) * places], total)
            chosen.append(total)
        packed[...] = jnp.concatenate(chosen, axis=0).T
        home_sums[...] += split_dot(home_right, home_left, 2)

    def add_to_slots(slots, values_of):
        hot_groups = []
        weighted = []
        for slot, values in zip(slots, values_of):
            index = slot.astype(I32)
            hot_groups.append(hot_rows(groups, lax.shift_right_logical(index, 7).astype(F32)))
            lane_row = jnp.bitwise_and(index, LANES - 1).astype(F32)
            mask = count[:LANES] == spread_rows(lane_row, LANES)
            weighted.append(
                jnp.concatenate(
                    [jnp.where(mask, spread_rows(v, LANES), BF16(0)) for v in values], axis=0
                )
            )
        hist[...] += nt_dot(side_by_side(hot_groups), side_by_side(weighted))

    def stray_sums(size):
        hot = side_by_side([hot_rows(label_groups, row_of(packed, q)) for q in range(size)])
        found = jnp.dot(
            table[...], jnp.concatenate([hot] * (1 + digits), axis=0), preferred_element_type=F32
        )
        slots = []
        for q in range(size):
            mask = iota((LANES, LANES), 0) == row_of(packed, size + q).astype(I32)
            slots.append(
                jnp.sum(
                    jnp.where(mask, found[:, q * LANES : (q + 1) * LANES], 0.0),
                    axis=0, keepdims=True,
                )
            )
        return slots, [[row_of(packed, (2 + i) * size + q) for i in range(4)] for q in range(size)]

    def home_totals():
        homes_t = home_sums[...].T
        for which in range(2):
            low = 2 * which * home_rows
            value = (homes_t[low : low + home_rows] + homes_t[low + home_rows : low + 2 * home_rows])
            high = value.astype(BF16).astype(F32)
            home_parts[2 * which] = high
            home_parts[2 * which + 1] = value - high
        return (
            [row_of(slot_tab, first_group + i) for i in range(window)],
            [[home_parts[k, pl.ds(i, 1), :] for k in range(4)] for i in range(window)],
        )

    chunks = rows // ROWS_AT_ONCE

    def inner_chunk(chunk, unused):
        add_to_slots(*stray_sums(BATCH))
        compact(chunk * BATCH if isinstance(chunk, int) else pl.multiple_of(chunk * BATCH, 8), BATCH)
        return unused

    prepare()
    steps = (rows - ROWS_AT_ONCE) // BATCH
    early = min(EARLY, steps)
    compact(0, BATCH)
    add_to_slots(*stray_sums(BATCH))
    pl.semaphore_wait(barrier, blocks - 1 + len(near))
    start_halos()
    compact(BATCH, BATCH)
    lax.fori_loop(early, steps, inner_chunk, 0)
    held_rows = BATCH
    for base in range(steps * BATCH, rows - ROWS_AT_ONCE, ROWS_AT_ONCE):
        add_to_slots(*stray_sums(held_rows))
        compact(base, ROWS_AT_ONCE)
        held_rows = ROWS_AT_ONCE
    for load in loads[5:]:
        load.wait()

    def pair_copy():
        return pltpu.make_async_remote_copy(
            src_ref=sums.at[1 - side],
            dst_ref=pair,
            send_sem=one_send,
            recv_sem=one_recv,
            device_id=(b, t + 1 - 2 * side),
            device_id_type=MESH,
        )

    def two_copy(k):
        other, device = peer(k)
        return pltpu.make_async_remote_copy(
            src_ref=part.at[other],
            dst_ref=recv2.at[k - 1],
            send_sem=two_send.at[k - 1],
            recv_sem=two_recv.at[k - 1],
            device_id=device,
            device_id_type=MESH,
        )

    take_halos()
    add_to_slots(*stray_sums(held_rows))
    edges()
    compact(rows - ROWS_AT_ONCE, ROWS_AT_ONCE)
    strays, homes = stray_sums(ROWS_AT_ONCE), home_totals()
    add_to_slots(strays[0] + homes[0], strays[1] + homes[1])
    for which in range(2):
        low = 2 * which * LANES
        total = hist[:, pl.ds(low, LANES)] + hist[:, pl.ds(low + LANES, LANES)]
        total = total.reshape(blocks, 2, gp, LANES)
        for p in range(2):
            sums[p, :, which] = total[:, p]
    pair_copy().start()
    rest = adj_f[...]
    for piece in range(3):
        high = rest.astype(BF16)
        adj0[pl.ds(piece * rows, rows)] = high
        rest = rest - high.astype(F32)
    pair_copy().wait()
    part[...] = sums[side] + pair[...]
    for k in range(1, blocks):
        two_copy(k).start()
    reaches, chains = cell_in.shape
    shift = cols.bit_length() - 1

    def levees(chunk, unused):
        base = chunk * 4
        cells = jnp.concatenate([row_of(cell_in, base + q) for q in range(4)], axis=1)
        wide = 4 * chains
        column = jnp.bitwise_and(cells, cols - 1)
        line = lax.shift_right_logical(cells, shift)
        hot = jnp.where(iota((cols, wide), 0) == column, 1.0, 0.0).astype(BF16)
        picked = jnp.dot(adj0[...], hot, preferred_element_type=F32)
        picked = (picked[:rows] + picked[rows : 2 * rows]) + picked[2 * rows :]
        value = jnp.sum(
            jnp.where(iota((rows, wide), 0) == line, picked, 0.0), axis=0, keepdims=True
        )
        for q in range(4):
            levee[pl.ds(base + q, 1), :] = value[:, q * chains : (q + 1) * chains]
        return unused

    lax.fori_loop(0, reaches // 4, levees, 0)

    rate = keep_in[...]
    push = force_in[...] + levee_gain * levee[...]
    reach_id = iota((reaches, chains), 0)
    step = 1
    while step < reaches:
        has = reach_id < reaches - step
        next_rate = jnp.where(has, pltpu.roll(rate, reaches - step, 0), 1.0)
        next_push = jnp.where(has, pltpu.roll(push, reaches - step, 0), 0.0)
        push = push + rate * next_push
        rate = rate * next_rate
        step *= 2
    maps[0, pl.ds(0, 1)] = rate[0:1]
    maps[0, pl.ds(1, 1)] = push[0:1]
    maps[0, pl.ds(2, 6)] = jnp.zeros((6, chains), F32)

    def map_copy(k):
        return pltpu.make_async_remote_copy(
            src_ref=maps.at[0],
            dst_ref=maps.at[k],
            send_sem=map_send.at[k - 1],
            recv_sem=map_recv.at[k - 1],
            device_id=(lax.rem(b + k, nb), t),
            device_id_type=MESH,
        )

    for k in range(1, nb):
        map_copy(k).start()

    for k in range(1, nb):
        map_copy(k).wait()
    incoming = jnp.zeros((1, chains), F32)
    for other in reversed(range(nb)):
        slot = lax.rem(b - other + nb, nb)
        stretch = maps[slot]
        incoming = jnp.where(
            other > b, stretch[0:1] * incoming + stretch[1:2], incoming
        )
    packed_out[pl.ds(2 * gp, reaches)] = rate * incoming + push
    total = part[mine]
    for k in range(1, blocks):
        two_copy(k).wait()
        total = total + recv2[k - 1]
    for which in range(2):
        packed_out[pl.ds(which * gp, gp)] = total[which]


def full_kernel(
    nb, nt, span, gp, digits,
    depth_in, rough_in, seed_in, label_hbm, owner_hbm, keep_hbm, force_hbm, cell_hbm,
    packed_out,
    label_in, owner_in, keep_in, force_in, cell_in, ext, table, owner_f, slot_s, pieces, diff_e, diff_s, adj0, levee,
    hist, sums, recv1, part, recv2, maps,
    halo_send, halo_recv, map_send, map_recv, one_send, one_recv, two_send, two_recv, load_sem,
):
    b = lax.axis_index("basin")
    t = lax.axis_index("tile")
    rows, cols = depth_in.shape
    label_groups = table.shape[1] // (1 + digits)
    groups = nb * nt * gp

    barrier = pltpu.get_barrier_semaphore()
    for k in range(1, nb):
        pl.semaphore_signal(
            barrier, inc=1, device_id=(lax.rem(b + k, nb), t), device_id_type=MESH
        )
    for k in range(1, nt):
        pl.semaphore_signal(
            barrier, inc=1, device_id=(b, lax.rem(t + k, nt)), device_id_type=MESH
        )

    fields = (depth_in, rough_in, seed_in)
    pairs = (
        (owner_hbm, owner_in), (label_hbm, label_in),
        (depth_in, ext.at[0, pl.ds(HALO, rows)]), (rough_in, ext.at[1, pl.ds(HALO, rows)]),
        (seed_in, ext.at[2, pl.ds(HALO, rows)]),
        (cell_hbm, cell_in), (keep_hbm, keep_in), (force_hbm, force_in),
    )
    loads = [
        pltpu.make_async_copy(source, target, load_sem.at[index])
        for index, (source, target) in enumerate(pairs)
    ]
    for load in loads:
        load.start()
    pl.semaphore_wait(barrier, nb - 1 + nt - 1)

    def down_copy(f):
        return pltpu.make_async_remote_copy(
            src_ref=fields[f].at[pl.ds(rows - HALO, HALO)],
            dst_ref=ext.at[f, pl.ds(0, HALO)],
            send_sem=halo_send.at[0, f],
            recv_sem=halo_recv.at[0, f],
            device_id=(b, lax.rem(t + 1, nt)),
            device_id_type=MESH,
        )

    def up_copy(f):
        return pltpu.make_async_remote_copy(
            src_ref=fields[f].at[pl.ds(0, HALO)],
            dst_ref=ext.at[f, pl.ds(HALO + rows, HALO)],
            send_sem=halo_send.at[1, f],
            recv_sem=halo_recv.at[1, f],
            device_id=(b, lax.rem(t + nt - 1, nt)),
            device_id_type=MESH,
        )

    @pl.when(t < nt - 1)
    def _():
        for f in range(3):
            down_copy(f).start()

    @pl.when(t > 0)
    def _():
        for f in range(3):
            up_copy(f).start()

    loads[0].wait()
    owner = owner_in[...].astype(F32)
    device = jnp.floor((owner + 0.5) * (1.0 / span))
    inside = owner - device * span
    block = jnp.floor(inside * (1.0 / LANES))
    group = device * gp + block
    lane = inside - block * LANES
    owner_f[...] = jnp.zeros(owner_f.shape, F32)
    held = owner.shape[0]
    parts = [lane]
    for digit in range(digits):
        upper = jnp.floor(group * (1.0 / 256.0))
        parts.append((group - upper * 256.0) * float(LANES * 256**digit))
        group = upper
    for index, value in enumerate(parts):
        owner_f[pl.ds(0, held)] = value
        table[:, pl.ds(index * label_groups, label_groups)] = owner_f[...].T.astype(BF16)
    count = iota((256, LANES), 0).astype(F32).astype(BF16)

    def spread_rows(row, size):
        tall = jnp.broadcast_to(row, (16, LANES)).astype(BF16)
        return jnp.concatenate([tall] * (size // 16), axis=0)

    def row_of(ref, row):
        return ref[pl.ds(row, 1), :]

    def hot_rows(size, index):
        if size > 256:
            return jnp.where(iota((size, cols), 0) == index, 1.0, 0.0).astype(BF16)
        narrow = index.astype(F32)
        return jnp.concatenate(
            [
                jnp.where(
                    count[:size] == spread_rows(narrow[:, c : c + LANES], size), BF16(1), BF16(0)
                )
                for c in range(0, cols, LANES)
            ],
            axis=1,
        )

    def look_up(chunk, unused):
        for q in range(ROWS_AT_ONCE):
            row = chunk * ROWS_AT_ONCE + q
            labels = row_of(label_in, row)
            hot = hot_rows(label_groups, lax.shift_right_logical(labels, 7))
            found = jnp.dot(
                table[...],
                jnp.concatenate([hot] * (1 + digits), axis=0),
                preferred_element_type=F32,
            )
            mask = iota((LANES, cols), 0) == jnp.bitwise_and(labels, LANES - 1)
            slot_s[pl.ds(row, 1), :] = jnp.sum(
                jnp.where(mask, found, 0.0), axis=0, keepdims=True
            )
        return unused

    loads[1].wait()
    lax.fori_loop(0, rows // ROWS_AT_ONCE, look_up, 0)
    for load in loads[2:]:
        load.wait()

    @pl.when(t < nt - 1)
    def _():
        for f in range(3):
            down_copy(f).wait_send()
            up_copy(f).wait_recv()

    @pl.when(t > 0)
    def _():
        for f in range(3):
            up_copy(f).wait_send()
            down_copy(f).wait_recv()

    @pl.when(t == 0)
    def _():
        for f in range(3):
            ext[f, pl.ds(0, HALO)] = jnp.ones((HALO, cols), F32)

    @pl.when(t == nt - 1)
    def _():
        for f in range(3):
            ext[f, pl.ds(HALO + rows, HALO)] = jnp.ones((HALO, cols), F32)

    deep = rows + 2 * HALO
    row_id = iota((deep, cols), 0)
    col_id = iota((deep, cols), 1)
    first = jnp.where(t == 0, HALO, 0)
    last = jnp.where(t == nt - 1, HALO + rows - 1, deep - 1)
    inner = (row_id >= first) & (row_id <= last)
    face_s = (row_id >= first) & (row_id < last)
    face_e = col_id < cols - 1

    def below(v):
        return pltpu.roll(v, deep - 1, 0)

    def right(v):
        return pltpu.roll(v, cols - 1, 1)

    def from_above(v):
        return pltpu.roll(v, 1, 0)

    def from_left(v):
        return pltpu.roll(v, 1, 1)

    conduct = jnp.where(inner, rough_ref / ext[1], 0.0)
    weight_e = jnp.where(face_e, (0.5 * courant) * (conduct + right(conduct)), 0.0)
    weight_s = jnp.where(face_s, (0.5 * courant) * (conduct + below(conduct)), 0.0)

    def advance(v, de, ds):
        flow_e = weight_e * de
        flow_s = weight_s * ds
        return v + ((flow_e - from_left(flow_e)) + (flow_s - from_above(flow_s)))

    depth = ext[0]
    for s in range(STEPS):
        de = right(depth) - depth
        ds = below(depth) - depth
        diff_e[s] = de
        diff_s[s] = ds
        if s < STEPS - 1:
            depth = advance(depth, de, ds)
    adjoint = ext[2]
    prod_e = jnp.zeros((deep, cols), F32)
    prod_s = jnp.zeros((deep, cols), F32)
    for s in reversed(range(STEPS)):
        de = right(adjoint) - adjoint
        ds = below(adjoint) - adjoint
        prod_e = prod_e + diff_e[s] * de
        prod_s = prod_s + diff_s[s] * ds
        adjoint = advance(adjoint, de, ds)
    prod_e = jnp.where(face_e, prod_e, 0.0)
    prod_s = jnp.where(face_s, prod_s, 0.0)
    product = (prod_e + from_left(prod_e)) + (prod_s + from_above(prod_s))
    gradient = ((0.5 * courant) * conduct * product)[HALO : HALO + rows]
    square = gradient * gradient
    for index, value in enumerate((gradient, square)):
        high = value.astype(BF16).astype(F32)
        pieces[2 * index] = high
        pieces[2 * index + 1] = value - high

    def gather_rows(which, chunk, unused):
        hot_groups = []
        weighted = []
        for q in range(ROWS_AT_ONCE):
            row = chunk * ROWS_AT_ONCE + q
            slot = row_of(slot_s, row).astype(I32)
            hot_groups.append(hot_rows(groups, lax.shift_right_logical(slot, 7)))
            lane_row = jnp.bitwise_and(slot, LANES - 1).astype(F32)
            values = [pieces[i, pl.ds(row, 1), :] for i in range(4)]
            masked = []
            for c in range(0, cols, LANES):
                mask = count[:LANES] == spread_rows(lane_row[:, c : c + LANES], LANES)
                masked.append(
                    jnp.concatenate(
                        [
                            jnp.where(mask, spread_rows(v[:, c : c + LANES], LANES), BF16(0))
                            for v in values
                        ],
                        axis=0,
                    )
                )
            weighted.append(jnp.concatenate(masked, axis=1))
        hist[...] += nt_dot(
            jnp.concatenate(weighted, axis=1), jnp.concatenate(hot_groups, axis=1)
        )
        return unused

    chunks = rows // ROWS_AT_ONCE

    def one_copy(which, k):
        other = lax.rem(b + k, nb)
        return pltpu.make_async_remote_copy(
            src_ref=sums.at[which, pl.ds(pl.multiple_of(other * (nt * gp), 8), nt * gp)],
            dst_ref=recv1.at[k - 1, which],
            send_sem=one_send.at[which, k - 1],
            recv_sem=one_recv.at[which, k - 1],
            device_id=(other, t),
            device_id_type=MESH,
        )

    def two_copy(which, k):
        other = lax.rem(t + k, nt)
        return pltpu.make_async_remote_copy(
            src_ref=part.at[which, pl.ds(pl.multiple_of(other * gp, 8), gp)],
            dst_ref=recv2.at[k - 1, which],
            send_sem=two_send.at[which, k - 1],
            recv_sem=two_recv.at[which, k - 1],
            device_id=(b, other),
            device_id_type=MESH,
        )

    def collect(which, start, stop):
        lax.fori_loop(start, stop, functools.partial(gather_rows, which), 0)

    def first_phase(which):
        sums[which] = (hist[pl.ds(2 * which * LANES, LANES)] + hist[pl.ds((2 * which + 1) * LANES, LANES)]).T
        for k in range(1, nb):
            one_copy(which, k).start()

    def second_phase(which):
        for k in range(1, nb):
            one_copy(which, k).wait()
        total = sums[which, pl.ds(pl.multiple_of(b * (nt * gp), 8), nt * gp)]
        for k in range(1, nb):
            total = total + recv1[k - 1, which]
        part[which] = total
        for k in range(1, nt):
            two_copy(which, k).start()

    def finish(which):
        for k in range(1, nt):
            two_copy(which, k).wait()
        total = part[which, pl.ds(pl.multiple_of(t * gp, 8), gp)]
        for k in range(1, nt):
            total = total + recv2[k - 1, which]
        packed_out[pl.ds(which * gp, gp)] = total

    hist[...] = jnp.zeros(hist.shape, F32)
    collect(0, 0, chunks)
    first_phase(0)
    first_phase(1)
    rest = adjoint[HALO : HALO + rows]
    for piece in range(3):
        high = rest.astype(BF16)
        adj0[pl.ds(piece * rows, rows)] = high
        rest = rest - high.astype(F32)
    reaches, chains = cell_in.shape
    shift = cols.bit_length() - 1

    def levees(chunk, unused):
        base = chunk * 4
        cells = jnp.concatenate([row_of(cell_in, base + q) for q in range(4)], axis=1)
        wide = 4 * chains
        column = jnp.bitwise_and(cells, cols - 1)
        line = lax.shift_right_logical(cells, shift)
        hot = jnp.where(iota((cols, wide), 0) == column, 1.0, 0.0).astype(BF16)
        picked = jnp.dot(adj0[...], hot, preferred_element_type=F32)
        picked = (picked[:rows] + picked[rows : 2 * rows]) + picked[2 * rows :]
        value = jnp.sum(
            jnp.where(iota((rows, wide), 0) == line, picked, 0.0), axis=0, keepdims=True
        )
        for q in range(4):
            levee[pl.ds(base + q, 1), :] = value[:, q * chains : (q + 1) * chains]
        return unused

    lax.fori_loop(0, reaches // 4, levees, 0)

    rate = keep_in[...]
    push = force_in[...] + levee_gain * levee[...]
    reach_id = iota((reaches, chains), 0)
    step = 1
    while step < reaches:
        has = reach_id < reaches - step
        next_rate = jnp.where(has, pltpu.roll(rate, reaches - step, 0), 1.0)
        next_push = jnp.where(has, pltpu.roll(push, reaches - step, 0), 0.0)
        push = push + rate * next_push
        rate = rate * next_rate
        step *= 2
    maps[0, pl.ds(0, 1)] = rate[0:1]
    maps[0, pl.ds(1, 1)] = push[0:1]
    maps[0, pl.ds(2, 6)] = jnp.zeros((6, chains), F32)

    def map_copy(k):
        return pltpu.make_async_remote_copy(
            src_ref=maps.at[0],
            dst_ref=maps.at[k],
            send_sem=map_send.at[k - 1],
            recv_sem=map_recv.at[k - 1],
            device_id=(lax.rem(b + k, nb), t),
            device_id_type=MESH,
        )

    for k in range(1, nb):
        map_copy(k).start()

    second_phase(0)
    second_phase(1)
    for k in range(1, nb):
        map_copy(k).wait()
    incoming = jnp.zeros((1, chains), F32)
    for other in reversed(range(nb)):
        slot = lax.rem(b - other + nb, nb)
        stretch = maps[slot]
        incoming = jnp.where(
            other > b, stretch[0:1] * incoming + stretch[1:2], incoming
        )
    packed_out[pl.ds(2 * gp, reaches)] = rate * incoming + push
    finish(0)
    finish(1)


def unpack(gp, packed_in, grad_out, curv_out, reach_out):
    grad_out[...] = packed_in[pl.ds(0, gp)]
    curv_out[...] = packed_in[pl.ds(gp, gp)]
    reach_out[...] = packed_in[pl.ds(2 * gp, reach_out.shape[0])]


def full_pass(
    nb, nt, gp, depth_start, roughness, depth_seed, zone_label, owner_slot, retention, forcing,
    levee_cell,
):
    zones = owner_slot.shape[0]
    span = zones // (nb * nt)
    groups = nb * nt * gp
    digits = 1 if groups <= 256 else 2
    rows, cols = depth_start.shape[1:]
    reaches, chains = retention.shape
    padded = round_up(zones, LANES)
    owner = jnp.pad(owner_slot, (0, padded - zones)).reshape(-1, LANES)
    label_groups = round_up(owner.shape[0], LANES)
    deep = rows + 2 * HALO
    vmem = pl.BlockSpec(memory_space=pltpu.VMEM)
    dma = pltpu.SemaphoreType.DMA
    return pl.pallas_call(
        functools.partial(full_kernel, nb, nt, span, gp, digits),
        out_shape=jax.ShapeDtypeStruct((2 * gp + reaches, LANES), F32),
        in_specs=[pl.BlockSpec(memory_space=pl.ANY)] * 8,
        out_specs=vmem,
        scratch_shapes=[
            pltpu.VMEM((rows, cols), I32),
            pltpu.VMEM(owner.shape, I32),
            pltpu.VMEM((reaches, chains), F32),
            pltpu.VMEM((reaches, chains), F32),
            pltpu.VMEM((reaches, chains), I32),
            pltpu.VMEM((3, deep, cols), F32),
            pltpu.VMEM((LANES, (1 + digits) * label_groups), BF16),
            pltpu.VMEM((label_groups, LANES), F32),
            pltpu.VMEM((rows, cols), F32),
            pltpu.VMEM((4, rows, cols), F32),
            pltpu.VMEM((STEPS, deep, cols), F32),
            pltpu.VMEM((STEPS, deep, cols), F32),
            pltpu.VMEM((3 * rows, cols), BF16),
            pltpu.VMEM((reaches, chains), F32),
            pltpu.VMEM((4 * LANES, groups), F32),
            pltpu.VMEM((2, groups, LANES), F32),
            pltpu.VMEM((nb - 1, 2, nt * gp, LANES), F32),
            pltpu.VMEM((2, nt * gp, LANES), F32),
            pltpu.VMEM((nt - 1, 2, gp, LANES), F32),
            pltpu.VMEM((nb, 8, chains), F32),
            dma((2, 3)), dma((2, 3)),
            dma((nb - 1,)), dma((nb - 1,)),
            dma((2, nb - 1)), dma((2, nb - 1)),
            dma((2, nt - 1)), dma((2, nt - 1)),
            dma((8,)),
        ],
        compiler_params=pltpu.CompilerParams(collective_id=1, has_side_effects=True),
    )(
        depth_start[0], roughness[0], depth_seed[0], zone_label[0], owner, retention, forcing,
        levee_cell,
    )


def per_device(
    nb, nt, depth_start, roughness, depth_seed, zone_label, owner_slot, retention, forcing,
    levee_cell,
):
    zones = owner_slot.shape[0]
    span = zones // (nb * nt)
    gp = round_up(round_up(span + 1, LANES) // LANES, 8)
    window = (span + LANES - 2) // LANES + 1
    home_rows = round_up(window, 16)
    groups = nb * nt * gp
    digits = 1 if groups <= 256 else 2
    blocks = nb * nt // 2
    rows, cols = depth_start.shape[1:]
    reaches, chains = retention.shape
    padded = round_up(zones, LANES)
    owner = jnp.pad(owner_slot, (0, padded - zones)).reshape(-1, LANES)
    label_groups = round_up(owner.shape[0], LANES)
    deep = rows + 2 * HALO
    vmem = pl.BlockSpec(memory_space=pltpu.VMEM)
    dma = pltpu.SemaphoreType.DMA
    packed = pl.pallas_call(
        functools.partial(main_kernel, nb, nt, span, gp, digits, window),
        out_shape=jax.ShapeDtypeStruct((2 * gp + reaches, LANES), F32),
        in_specs=[pl.BlockSpec(memory_space=pl.ANY)] * 8,
        out_specs=vmem,
        scratch_shapes=[
            pltpu.VMEM((rows, cols), I32),
            pltpu.VMEM(owner.shape, I32),
            pltpu.VMEM((reaches, chains), F32),
            pltpu.VMEM((reaches, chains), F32),
            pltpu.VMEM((reaches, chains), I32),
            pltpu.VMEM((3, deep, cols), F32),
            pltpu.VMEM((LANES, (1 + digits) * label_groups), BF16),
            pltpu.VMEM((label_groups, LANES), F32),
            pltpu.VMEM((label_groups + home_rows, LANES), F32),
            pltpu.VMEM((4, rows, cols), F32),
            pltpu.VMEM((4, rows, cols), F32),
            pltpu.VMEM((LANES, LANES), F32),
            pltpu.VMEM((LANES, 4 * home_rows), F32),
            pltpu.VMEM((4, home_rows, LANES), F32),
            pltpu.VMEM((STEPS, rows, cols), F32),
            pltpu.VMEM((STEPS, rows, cols), F32),
            pltpu.VMEM((rows, cols), F32),
            pltpu.VMEM((3 * rows, cols), BF16),
            pltpu.VMEM((reaches, chains), F32),
            pltpu.VMEM((groups, 4 * LANES), F32),
            pltpu.VMEM((2, blocks, 2, gp, LANES), F32),
            pltpu.VMEM((blocks, 2, gp, LANES), F32),
            pltpu.VMEM((blocks, 2, gp, LANES), F32),
            pltpu.VMEM((blocks - 1, 2, gp, LANES), F32),
            pltpu.VMEM((nb, 8, chains), F32),
            dma((2, 3)), dma((2, 3)),
            dma((nb - 1,)), dma((nb - 1,)),
            dma, dma,
            dma((blocks - 1,)), dma((blocks - 1,)),
            dma((8,)),
        ],
        compiler_params=pltpu.CompilerParams(collective_id=0, has_side_effects=True),
    )(
        depth_start[0], roughness[0], depth_seed[0], zone_label[0], owner, retention, forcing,
        levee_cell,
    )

    def unpack_with(words, value):
        return pl.pallas_call(
            functools.partial(unpack, words),
            out_shape=(
                jax.ShapeDtypeStruct((words, LANES), F32),
                jax.ShapeDtypeStruct((words, LANES), F32),
                jax.ShapeDtypeStruct((reaches, chains), F32),
            ),
            in_specs=[vmem],
            out_specs=(vmem,) * 3,
        )(value)

    def crowded(value):
        again = full_pass(
            nb, nt, gp, depth_start, roughness, depth_seed, zone_label, owner_slot, retention,
            forcing, levee_cell,
        )
        return unpack_with(gp, again)

    grad, curv, reach = lax.cond(
        packed[gp - 1, LANES - 1] > 0.5, crowded, functools.partial(unpack_with, gp), packed
    )
    return grad.reshape(-1)[:span], curv.reshape(-1)[:span], reach


def solution(mesh):
    in_specs = (
        P("basin", "tile", None),
        P("basin", "tile", None),
        P("basin", "tile", None),
        P("basin", "tile", None),
        P(),
        P("basin", "tile"),
        P("basin", "tile"),
        P("basin", "tile"),
    )
    out_specs = (P(("basin", "tile")), P(("basin", "tile")), P("basin", "tile"))
    return jax.shard_map(
        functools.partial(per_device, mesh.shape["basin"], mesh.shape["tile"]),
        mesh=mesh, in_specs=in_specs, out_specs=out_specs, check_vma=False,
    )
```
